128 devices in a mesh: member: 16 (over z_lo, y, core), band: 8 (over x, z_hi).
Axes of the slice: x: 4, y: 4, z: 4 (z_hi: 2, z_lo: 2; z = z_hi * 2 + z_lo), core: 2. Of those that a mesh axis runs over, the one named last changes fastest.
Arguments:
- height_start: float32 [80, 512, 1024], P(None, 'member', 'band'), may hold values from -6 to 6
- east_start: float32 [80, 512, 1024], P(None, 'member', 'band'), may hold values from -6 to 6
- north_start: float32 [80, 512, 1024], P(None, 'member', 'band'), may hold values from -6 to 6
- obs_value: float32 [512, 1024], P('member', 'band'), may hold values from -8 to 8
- obs_mask: int32 [512, 1024], P('member', 'band'), may hold values 0 or 1
- obs_precision: float32 [512, 1024], P('member', 'band'), may hold values from 0.25 to 4
- step_sizes: int32 [2], replicated, may hold values from 4 to 12
Outputs:
- analysis_height: float32 [80, 512, 1024], P(None, 'member', 'band')
- analysis_east: float32 [80, 512, 1024], P(None, 'member', 'band')
- analysis_north: float32 [80, 512, 1024], P(None, 'member', 'band')
The draws below stay inside these ranges and needn't reach their ends.
All inputs are finite; a program needn't handle non-finite values. No bound on the sum of `obs_mask` on one device may be relied on, other than what follows from the above.
Results may differ from the reference program's by a relative error of at most 0.0001.
Values sent between devices are 32-bit elements; how exact they have to be, the bound alone decides.
A program may use at most 128 MiB of HBM per device.

```python
import math
import jax
import jax.numpy as jnp
from jax import lax

MEMBERS = 80
STEPS = 3
ITERS = 2
LWIDTH = 32
LSCALE = 12
LAT = 512
LON = 1024


def with_ends(values, stream_key, least, largest):
    dims = values.shape
    spot = [jax.random.randint(jax.random.fold_in(stream_key, axis), (), 0, dims[axis]) for axis in range(len(dims))]
    values = values.at[tuple(spot)].set(least)
    longest = dims.index(max(dims))
    spot[longest] = (spot[longest] + 1) % dims[longest]
    return values.at[tuple(spot)].set(largest)


def block_scale(rng, shape, pieces, smallest, top_value):
    loudness, own = 1.0, jax.random.fold_in(rng, 6)
    for position, shards_of in pieces:
        heights = jnp.exp(jax.random.uniform(jax.random.fold_in(own, position), (shards_of,), jnp.float32, smallest / len(pieces), top_value / len(pieces)))
        loudness = loudness * jnp.repeat(heights, shape[position] // shards_of).reshape([-1 if axis == position else 1 for axis in range(len(shape))])
    return loudness


def normal_values(rng, extent, scale, limit, pieces=(), kind=jnp.bfloat16):
    loudness = block_scale(rng, extent, pieces, -0.22, 0.18) if pieces else 1.0
    values = jax.random.normal(rng, extent, jnp.float32) * scale * loudness
    return jnp.minimum(jnp.maximum(values, -limit), limit).astype(kind)


def setup_inputs(seed: int = 0) -> dict:
    seeds = jax.random.split(jax.random.key(seed), 8)
    height_start = normal_values(seeds[0], (MEMBERS, LAT, LON), 1.0, 6.0, ((1, 16), (2, 8)), jnp.float32)
    east_start = normal_values(seeds[1], (MEMBERS, LAT, LON), 1.0, 6.0, ((1, 16), (2, 8)), jnp.float32)
    north_start = normal_values(seeds[2], (MEMBERS, LAT, LON), 1.0, 6.0, ((1, 16), (2, 8)), jnp.float32)
    obs_value = normal_values(seeds[3], (LAT, LON), 1.5, 8.0, ((0, 16), (1, 8)), jnp.float32)
    obs_mask = with_ends((jax.random.randint(seeds[4], (LAT, LON), 0, 2) < 1).astype(jnp.int32), jax.random.fold_in(seeds[4], 1), 0, 1)
    obs_precision = jnp.clip(jnp.exp(math.log(4.0) - 2.7725887 * jax.random.uniform(seeds[5], (LAT, LON), jnp.float32) ** block_scale(seeds[5], (LAT, LON), ((0, 16), (1, 8)), -0.2, 0.2)), 0.25, 4.0)
    step_sizes = jax.random.randint(seeds[6], (ITERS,), 4, 13).astype(jnp.int32)
    return {"height_start": height_start, "east_start": east_start, "north_start": north_start, "obs_value": obs_value, "obs_mask": obs_mask, "obs_precision": obs_precision, "step_sizes": step_sizes}


highest = lax.Precision.HIGHEST

def taper_kernel(outputs, inputs, margin, spread):
    out_index = jnp.arange(outputs, dtype=jnp.int32)[:, None]
    in_index = jnp.arange(inputs, dtype=jnp.int32)[None, :]
    offset = (in_index - margin - out_index).astype(jnp.float32)
    scaled_off = offset / spread
    weight = jnp.exp(-0.5 * scaled_off * scaled_off)
    return jnp.where(jnp.abs(offset) <= margin, weight, jnp.zeros_like(weight))

def taper_rows(padded, row_count, margin, spread):
    kernel = taper_kernel(row_count, row_count + 2 * margin, margin, spread)
    return jnp.einsum('ab,mbc->mac', kernel, padded, precision=highest)

def taper_columns(padded, columns, margin, spread):
    block_size = 128 if columns % 128 == 0 else columns
    windows = jnp.stack([lax.slice_in_dim(padded, block_start, block_start + block_size + 2 * margin, axis=2) for block_start in range(0, columns, block_size)], axis=2)
    kernel = taper_kernel(block_size, block_size + 2 * margin, margin, spread)
    result = jnp.einsum('mrjk,bk->mrjb', windows, kernel, precision=highest)
    return result.reshape(padded.shape[0], padded.shape[1], columns)

def lon_diff(grid_field):
    return jnp.roll(grid_field, -1, axis=2) - jnp.roll(grid_field, 1, axis=2)

def lat_diff(grid_field):
    padded = jnp.pad(grid_field, ((0, 0), (1, 1), (0, 0)))
    return padded[:, 2:, :] - padded[:, :-2, :]

def advance(height, eastward, northward):
    new_height = height - 0.2 * (lon_diff(eastward) + lat_diff(northward))
    new_east = eastward + 0.1 * northward - 0.2 * lon_diff(new_height)
    new_north = northward - 0.1 * eastward - 0.2 * lat_diff(new_height)
    return (new_height, new_east, new_north)

def localize(contrib):
    margin = LWIDTH
    padded = jnp.pad(contrib, ((0, 0), (margin, margin), (0, 0)))
    lat_done = taper_rows(padded, contrib.shape[1], margin, LSCALE)
    wrapped = jnp.concatenate([lat_done[:, :, -margin:], lat_done, lat_done[:, :, :margin]], axis=2)
    return taper_columns(wrapped, contrib.shape[2], margin, LSCALE)

def member_sum(anomaly, weights):
    return lax.optimization_barrier(jnp.sum(anomaly * weights, axis=0))

def reference(height_start, east_start, north_start, obs_value, obs_mask, obs_precision, step_sizes):
    height, eastward, northward = (height_start, east_start, north_start)
    for section_number in range(STEPS):
        height, eastward, northward = advance(height, eastward, northward)
    members = height.shape[0]
    root_scale = jnp.sqrt(jnp.float32(members - 1))
    mean_height = lax.optimization_barrier(jnp.sum(height, axis=0)) / members
    mean_east = lax.optimization_barrier(jnp.sum(eastward, axis=0)) / members
    mean_north = lax.optimization_barrier(jnp.sum(northward, axis=0)) / members
    anom_height = (height - mean_height) / root_scale
    anom_east = (eastward - mean_east) / root_scale
    anom_north = (northward - mean_north) / root_scale
    obs_weight = obs_mask.astype(jnp.float32) * obs_precision
    weights = jnp.zeros_like(height)
    cell_total = float(members * height.shape[1] * height.shape[2])
    for iteration in range(ITERS):
        state_height = mean_height + member_sum(anom_height, weights)
        state_east = mean_east + member_sum(anom_east, weights)
        state_north = mean_north + member_sum(anom_north, weights)
        residual = obs_weight * (obs_value - state_height - 0.15 * (state_east * state_east + state_north * state_north))
        contrib = (anom_height + 0.3 * (state_east * anom_east + state_north * anom_north)) * residual
        gradient = weights - localize(contrib)
        square_total = jnp.sum(gradient * gradient)
        factor = step_sizes[iteration].astype(jnp.float32) / 64.0 / jnp.sqrt(square_total / cell_total + 1e-06)
        weights = weights - factor * gradient
    return (height + member_sum(anom_height, weights), eastward + member_sum(anom_east, weights), northward + member_sum(anom_north, weights))
```

```python
import functools
import math

import jax
import jax.numpy as jnp
from jax import lax
from jax.experimental import pallas as pl
from jax.experimental.pallas import tpu as pltpu
from jax.sharding import PartitionSpec as P

MESH = pl.DeviceIdType.MESH
F32 = jnp.float32
BF16 = jnp.bfloat16

MEMBERS = 80
ROWS = 32
COLS = 128
NMEM = 16
NBAND = 8
STEPS = 3
LSCALE = 12.0
REACH = 32
GROUPS = 11
MEAN = 80
CHUNK = 16
NCHUNK = MEMBERS // CHUNK
QUADS = CHUNK // 4
CELLS = float(MEMBERS * 512 * 1024)


def taper(offset):
    scaled = offset.astype(F32) / LSCALE
    weight = jnp.exp(-0.5 * scaled * scaled)
    return jnp.where(jnp.abs(offset) <= REACH, weight, 0.0)


def split(x):
    high = x.astype(BF16)
    low = (x - high.astype(F32)).astype(BF16)
    return high, low


def build_tapers(lat_k, lon_k):
    i = lax.broadcasted_iota(jnp.int32, (64, 192), 0)
    j = lax.broadcasted_iota(jnp.int32, (64, 192), 1)
    a = jnp.where(i < 32, i, i - 32)
    jj = jnp.where(j < 96, j, j - 96)
    w = taper(jj - 32 - a)
    high = w.astype(BF16).astype(F32)
    low = jnp.where(j < 96, w - high, 0.0)
    lat_k[...] = jnp.where(i < 32, high, low).astype(BF16)
    for s in range(4):
        for block in range(3):
            k = lax.broadcasted_iota(jnp.int32, (128, 256), 0)
            n = lax.broadcasted_iota(jnp.int32, (128, 256), 1)
            out = jnp.where(n < 128, n, n - 128)
            if block == 0:
                w = taper(k - out)
            else:
                inside = (k >= 32 * s) & (k < 32 * s + 32)
                start = -32 if block == 1 else 128
                w = jnp.where(inside, taper(k - 32 * s + start - out), 0.0)
            high = w.astype(BF16).astype(F32)
            lon_k[s, pl.ds(128 * block, 128), :] = jnp.where(n < 128, high, w - high).astype(BF16)


def kernel(
    h_in, u_in, v_in, obs_value, obs_mask, obs_precision, steps,
    h_out, u_out, v_out, inc,
    x, f, rh, ps, pr, c, rc, lt, ls, lr, g1, lat_k, lon_k, coef, state, s_acc, sq, red,
    load_sem, store_sem, halo_ss, halo_rs, row_ss, row_rs, col_ss, col_rs, red_ss, red_rs,
):
    m = lax.axis_index("member")
    b = lax.axis_index("band")
    has_up = m > 0
    has_dn = m < NMEM - 1
    up = lax.rem(m + NMEM - 1, NMEM)
    dn = lax.rem(m + 1, NMEM)
    lf = lax.rem(b + NBAND - 1, NBAND)
    rt = lax.rem(b + 1, NBAND)

    core = lax.rem(m, 2)
    y = lax.rem(m // 2, 4)
    z_lo = m // 8
    xx = b // 2
    z = lax.rem(b, 2) * 2 + z_lo

    def at(core_, y_, x_, z_):
        return ((lax.rem(z_, 2) * 4 + y_) * 2 + core_, x_ * 2 + z_ // 2)

    stages = [
        [at(1 - core, y, xx, z)],
        [at(core, lax.rem(y + j, 4), xx, z) for j in (1, 2, 3)],
        [at(core, y, lax.rem(xx + j, 4), z) for j in (1, 2, 3)],
        [at(core, y, xx, lax.rem(z + j, 4)) for j in (1, 2, 3)],
    ]

    near = [(up, b), (dn, b), (m, lf), (m, rt), (up, lf), (up, rt), (dn, lf), (dn, rt)]
    greet = near + [d for stage in stages for d in stage]
    barrier = pltpu.get_barrier_semaphore()
    for d in greet:
        pl.semaphore_signal(barrier, inc=1, device_id=d, device_id_type=MESH)

    loads = [
        pltpu.make_async_copy(src, x.at[k, pl.ds(0, MEMBERS)], load_sem.at[k])
        for k, src in enumerate((h_in, u_in, v_in))
    ]
    for copy in loads:
        copy.start()

    @pl.when(m == 0)
    def _():
        rh[:, 0] = jnp.zeros((3, 8 * GROUPS, 8, COLS), F32)
        pr[:, :, pl.ds(0, 8), :] = jnp.zeros((2, GROUPS, 8, COLS), F32)
        rc[0, 0] = jnp.zeros((MEMBERS, ROWS, COLS), F32)
        rc[1, 0] = jnp.zeros((MEMBERS, ROWS, COLS), F32)

    @pl.when(m == NMEM - 1)
    def _():
        rh[:, 1] = jnp.zeros((3, 8 * GROUPS, 8, COLS), F32)
        pr[:, :, pl.ds(40, 8), :] = jnp.zeros((2, GROUPS, 8, COLS), F32)
        rc[0, 1] = jnp.zeros((MEMBERS, ROWS, COLS), F32)
        rc[1, 1] = jnp.zeros((MEMBERS, ROWS, COLS), F32)

    build_tapers(lat_k, lon_k)
    x[:, pl.ds(MEAN + 1, 7)] = jnp.zeros((3, 7, ROWS, COLS), F32)

    for copy in loads:
        copy.wait()

    for k in range(3):
        x[k, MEAN] = lax.fori_loop(
            0, MEMBERS, lambda i, total, k=k: total + x[k, i], jnp.zeros((ROWS, COLS), F32), unroll=8
        ) * (1.0 / MEMBERS)

    lane = lax.broadcasted_iota(jnp.int32, (ROWS, COLS), 1)

    def pack(g):
        left = jnp.zeros((ROWS, COLS), F32)
        right = jnp.zeros((ROWS, COLS), F32)
        for s in range(8):
            base = 16 * s
            i = g * 8 + s
            for field, lo, width in ((1, 0, 6), (0, 6, 5), (2, 11, 5)):
                value = x[field, i]
                where = (lane >= base + lo) & (lane < base + lo + width)
                left = jnp.where(where, pltpu.roll(value, base + lo, 1), left)
                right = jnp.where(where, pltpu.roll(value, (base + lo + width) % COLS, 1), right)
        ps[0, g] = left
        ps[1, g] = right

    def halo_copy(k, g):
        members = pl.ds(g * 8, 8)
        top, bottom, body = pl.ds(0, 8), pl.ds(24, 8), pl.ds(8, 32)
        below = pl.ds(40, 8)
        src, dst = (
            (x.at[:, members, top], rh.at[:, 1, members]),
            (x.at[:, members, bottom], rh.at[:, 0, members]),
            (ps.at[0, g], pr.at[1, g, body]),
            (ps.at[1, g], pr.at[0, g, body]),
            (ps.at[0, g, top], pr.at[1, g, below]),
            (ps.at[1, g, top], pr.at[0, g, below]),
            (ps.at[0, g, bottom], pr.at[1, g, top]),
            (ps.at[1, g, bottom], pr.at[0, g, top]),
        )[k]
        return pltpu.make_async_remote_copy(
            src_ref=src, dst_ref=dst, send_sem=halo_ss.at[g, k], recv_sem=halo_rs.at[g, k],
            device_id=near[k], device_id_type=MESH,
        )

    def halo_start(g):
        @pl.when(has_up)
        def _():
            for k in (0, 4, 5):
                halo_copy(k, g).start()

        @pl.when(has_dn)
        def _():
            for k in (1, 6, 7):
                halo_copy(k, g).start()

        for k in (2, 3):
            halo_copy(k, g).start()

    def halo_wait(g):
        @pl.when(has_up)
        def _():
            for k in (1, 6, 7):
                halo_copy(k, g).wait_recv()
            for k in (0, 4, 5):
                halo_copy(k, g).wait_send()

        @pl.when(has_dn)
        def _():
            for k in (0, 4, 5):
                halo_copy(k, g).wait_recv()
            for k in (1, 6, 7):
                halo_copy(k, g).wait_send()

        for k in (2, 3):
            halo_copy(k, g).wait_recv()
            halo_copy(k, g).wait_send()

    pack(MEAN // 8)
    pl.semaphore_wait(barrier, len(greet))
    halo_start(MEAN // 8)

    def send_halo(g, carry):
        pack(g)
        halo_start(g)
        return carry

    lax.fori_loop(0, MEMBERS // 8, send_halo, 0)

    elane = lax.broadcasted_iota(jnp.int32, (48, COLS), 1)
    first, last, half = elane == 0, elane == COLS - 1, elane < 64
    erow = lax.broadcasted_iota(jnp.int32, (48, COLS), 0)
    inside = ((erow >= 8) | has_up) & ((erow < 40) | has_dn)

    def lon_diff(pair):
        main, side = pair
        em, es = pltpu.roll(main, COLS - 1, 1), pltpu.roll(side, COLS - 1, 1)
        wm, ws = pltpu.roll(main, 1, 1), pltpu.roll(side, 1, 1)
        return (
            jnp.where(last, es, em) - jnp.where(first, ws, wm),
            jnp.where(last, em, es) - jnp.where(first, wm, ws),
        )

    def lat_diff(pair):
        return tuple(pltpu.roll(q, 47, 0) - pltpu.roll(q, 1, 0) for q in pair)

    def forecast(g, s):
        i = g * 8 + s
        from_left, from_right = pr[0, g], pr[1, g]
        fields = []
        for k, lo, width in ((0, 6, 5), (1, 0, 6), (2, 11, 5)):
            main = jnp.concatenate([rh[k, 0, i], x[k, i], rh[k, 1, i]], axis=0)
            right = pltpu.roll(from_right, lax.rem(2 * COLS - lo - 16 * s, COLS), 1)
            left = pltpu.roll(from_left, lax.rem(2 * COLS - width - lo - 16 * s, COLS), 1)
            fields.append((main, jnp.where(half, right, left)))
        hh, uu, vv = fields
        for _ in range(STEPS):
            du, dv = lon_diff(uu), lat_diff(vv)
            hn = tuple(jnp.where(inside, hh[p] - 0.2 * (du[p] + dv[p]), 0.0) for p in range(2))
            dx, dy = lon_diff(hn), lat_diff(hn)
            un = tuple(uu[p] + 0.1 * vv[p] - 0.2 * dx[p] for p in range(2))
            vn = tuple(jnp.where(inside, vv[p] - 0.1 * uu[p] - 0.2 * dy[p], 0.0) for p in range(2))
            hh, uu, vv = hn, un, vn
        return hh[0][8:40], uu[0][8:40], vv[0][8:40]

    halo_wait(MEAN // 8)
    mean = forecast(MEAN // 8, 0)
    for k in range(3):
        state[k] = mean[k]
    obs_weight = obs_mask[...].astype(F32) * obs_precision[...]

    def set_coefficients(sh, su, sv):
        residual = obs_weight * (obs_value[...] - sh - 0.15 * (su * su + sv * sv))
        coef[0] = residual
        coef[1] = 0.3 * su * residual
        coef[2] = 0.3 * sv * residual

    set_coefficients(*mean)

    def row_copy(it, k, n):
        members = pl.ds(n * CHUNK, CHUNK)
        return pltpu.make_async_remote_copy(
            src_ref=c.at[members], dst_ref=rc.at[it, 1 - k, members],
            send_sem=row_ss.at[it, k, n], recv_sem=row_rs.at[it, k, n],
            device_id=near[k], device_id_type=MESH,
        )

    def row_start(it, n):
        @pl.when(has_up)
        def _():
            row_copy(it, 0, n).start()

        @pl.when(has_dn)
        def _():
            row_copy(it, 1, n).start()

    def row_wait(it, n):
        @pl.when(has_up)
        def _():
            row_copy(it, 1, n).wait_recv()

        @pl.when(has_dn)
        def _():
            row_copy(it, 0, n).wait_recv()

    def row_sent(it, n):
        @pl.when(has_up)
        def _():
            row_copy(it, 0, n).wait_send()

        @pl.when(has_dn)
        def _():
            row_copy(it, 1, n).wait_send()

    def col_copy(it, k, n):
        quads = pl.ds(n * QUADS, QUADS)
        return pltpu.make_async_remote_copy(
            src_ref=ls.at[k, quads], dst_ref=lr.at[it, 1 - k, quads],
            send_sem=col_ss.at[it, k, n], recv_sem=col_rs.at[it, k, n],
            device_id=near[2 + k], device_id_type=MESH,
        )

    scale = 1.0 / math.sqrt(MEMBERS - 1.0)

    def first_chunk(n, carry):
        for gg in range(CHUNK // 8):
            g = n * (CHUNK // 8) + gg
            halo_wait(g)

            def one(s, carry2, g=g):
                i = g * 8 + s
                out = forecast(g, s)
                total = None
                for k in range(3):
                    f[k, i] = out[k]
                    anomaly = (out[k] - state[k]) * scale
                    x[k, i] = anomaly
                    term = anomaly * coef[k]
                    total = term if total is None else total + term
                c[i] = total
                return carry2

            lax.fori_loop(0, 8, one, 0)
        row_start(0, n)
        return carry

    lax.fori_loop(0, NCHUNK, first_chunk, 0)

    stores = [
        pltpu.make_async_copy(f.at[k], dst, store_sem.at[k])
        for k, dst in enumerate((h_out, u_out, v_out))
    ]
    for copy in stores:
        copy.start()

    def taper_rows(it, n):
        row_wait(it, n)

        def quad(q, carry):
            parts_high, parts_low = [], []
            for ref_part in range(3):
                wide = []
                for s in range(4):
                    i = q * 4 + s
                    wide.append(rc[it, 0, i] if ref_part == 0 else (c[i] if ref_part == 1 else rc[it, 1, i]))
                high, low = split(jnp.concatenate(wide, axis=1))
                parts_high.append(high)
                parts_low.append(low)
            right_side = jnp.concatenate(parts_high + parts_low, axis=0)
            both = jnp.dot(lat_k[...], right_side, preferred_element_type=F32)
            lat = both[:32] + both[32:]
            to_left = jnp.zeros((ROWS, COLS), F32)
            to_right = jnp.zeros((ROWS, COLS), F32)
            for s in range(4):
                part = lat[:, s * COLS:(s + 1) * COLS]
                lt[s, q] = part
                where = (lane >= 32 * s) & (lane < 32 * s + 32)
                to_left = jnp.where(where, pltpu.roll(part, 32 * s, 1) if s else part, to_left)
                to_right = jnp.where(where, pltpu.roll(part, 32 * s + 32, 1) if s < 3 else part, to_right)
            ls[0, q] = to_left
            ls[1, q] = to_right
            return carry

        lax.fori_loop(n * QUADS, (n + 1) * QUADS, quad, 0)
        for k in range(2):
            col_copy(it, k, n).start()

    def taper_cols(it, n, factor):
        for k in range(2):
            col_copy(it, k, n).wait_recv()
        quads = pl.ds(n * QUADS, QUADS)
        size = QUADS * ROWS
        lh, ll = split(lr[it, 0, quads].reshape(size, COLS))
        rhh, rl = split(lr[it, 1, quads].reshape(size, COLS))
        totals = [None] * 4
        for s in range(4):
            mh, ml = split(lt[s, quads].reshape(size, COLS))
            a = jnp.dot(jnp.concatenate([mh, lh, rhh], axis=1), lon_k[s], preferred_element_type=F32)
            d = jnp.dot(jnp.concatenate([ml, ll, rl], axis=1), lon_k[s, :, pl.ds(0, 128)], preferred_element_type=F32)
            g = (a[:, :COLS] + a[:, COLS:] + d).reshape(QUADS, ROWS, COLS)
            if it == 0:
                g1[s, quads] = g
            else:
                g = factor * g1[s, quads] - g
            for qq in range(QUADS):
                i = (n * QUADS + qq) * 4 + s
                part = g[qq]
                terms = [x[k, i] * part for k in range(3)] + [part * part]
                totals = [t if o is None else o + t for o, t in zip(totals, terms)]
        for k in range(3):
            s_acc[it, k] += totals[k]
        sq[...] += totals[3]

    def localize(it, factor):
        def body(n, carry):
            @pl.when(n < NCHUNK)
            def _():
                taper_rows(it, n)

            @pl.when(n > 0)
            def _():
                taper_cols(it, n - 1, factor)

            return carry

        lax.fori_loop(0, NCHUNK + 1, body, 0)

    def sum_all(it):
        value = sq[...]
        value = value[:8] + value[8:16] + value[16:24] + value[24:]
        slot = 0
        for stage in stages:
            red[it, slot] = value
            copies = [
                pltpu.make_async_remote_copy(
                    src_ref=red.at[it, slot], dst_ref=red.at[it, slot + 1 + j],
                    send_sem=red_ss.at[it, slot + j], recv_sem=red_rs.at[it, slot + j],
                    device_id=d, device_id_type=MESH,
                )
                for j, d in enumerate(stage)
            ]
            for copy in copies:
                copy.start()
            for copy in copies:
                copy.wait_recv()
            for j in range(len(stage)):
                value = value + red[it, slot + 1 + j]
            for copy in copies:
                copy.wait_send()
            slot += 1 + len(stage)
        total = jnp.sum(jnp.sum(value, axis=0, keepdims=True), axis=1, keepdims=True)
        return steps[it].astype(F32) / 64.0 / jnp.sqrt(total / CELLS + 1e-6)

    for it in range(2):
        for k in range(3):
            s_acc[it, k] = jnp.zeros((ROWS, COLS), F32)
    sq[...] = jnp.zeros((ROWS, COLS), F32)
    localize(0, None)
    factor1 = sum_all(0)

    def sent(n, carry):
        row_sent(0, n)
        for k in range(2):
            col_copy(0, k, n).wait_send()
        return carry

    lax.fori_loop(0, NCHUNK, sent, 0)
    sq[...] = jnp.zeros((ROWS, COLS), F32)
    set_coefficients(*[state[k] + factor1 * s_acc[0, k] for k in range(3)])

    def second_chunk(n, carry):
        def one(j, carry2):
            i = n * CHUNK + j
            c[i] = x[0, i] * coef[0] + x[1, i] * coef[1] + x[2, i] * coef[2]
            return carry2

        lax.fori_loop(0, CHUNK, one, 0, unroll=4)
        row_start(1, n)
        return carry

    lax.fori_loop(0, NCHUNK, second_chunk, 0)
    localize(1, factor1)
    factor2 = sum_all(1)
    for k in range(3):
        inc[k] = factor1 * s_acc[0, k] - factor2 * s_acc[1, k]

    def sent2(n, carry):
        row_sent(1, n)
        for k in range(2):
            col_copy(1, k, n).wait_send()
        return carry

    lax.fori_loop(0, NCHUNK, sent2, 0)
    for copy in stores:
        copy.wait()


def per_device(height, east, north, obs_value, obs_mask, obs_precision, step_sizes):
    block = (MEMBERS, ROWS, COLS)
    vmem = pl.BlockSpec(memory_space=pltpu.VMEM)
    anyspace = pl.BlockSpec(memory_space=pl.ANY)
    dma = pltpu.SemaphoreType.DMA
    h, u, v, inc = pl.pallas_call(
        kernel,
        name="analysis",
        out_shape=[jax.ShapeDtypeStruct(block, F32)] * 3 + [jax.ShapeDtypeStruct((3, ROWS, COLS), F32)],
        in_specs=[anyspace] * 3 + [vmem] * 3 + [pl.BlockSpec(memory_space=pltpu.SMEM)],
        out_specs=[anyspace] * 3 + [vmem],
        scratch_shapes=[
            pltpu.VMEM((3, 8 * GROUPS, ROWS, COLS), F32),
            pltpu.VMEM((3, MEMBERS, ROWS, COLS), F32),
            pltpu.VMEM((3, 2, 8 * GROUPS, 8, COLS), F32),
            pltpu.VMEM((2, GROUPS, ROWS, COLS), F32),
            pltpu.VMEM((2, GROUPS, 48, COLS), F32),
            pltpu.VMEM(block, F32),
            pltpu.VMEM((2, 2) + block, F32),
            pltpu.VMEM((4, MEMBERS // 4, ROWS, COLS), F32),
            pltpu.VMEM((2, MEMBERS // 4, ROWS, COLS), F32),
            pltpu.VMEM((2, 2, MEMBERS // 4, ROWS, COLS), F32),
            pltpu.VMEM((4, MEMBERS // 4, ROWS, COLS), F32),
            pltpu.VMEM((64, 192), BF16),
            pltpu.VMEM((4, 384, 256), BF16),
            pltpu.VMEM((3, ROWS, COLS), F32),
            pltpu.VMEM((3, ROWS, COLS), F32),
            pltpu.VMEM((2, 3, ROWS, COLS), F32),
            pltpu.VMEM((ROWS, COLS), F32),
            pltpu.VMEM((2, 14, 8, COLS), F32),
            dma((3,)), dma((3,)),
            dma((GROUPS, 8)), dma((GROUPS, 8)),
            dma((2, 2, NCHUNK)), dma((2, 2, NCHUNK)),
            dma((2, 2, NCHUNK)), dma((2, 2, NCHUNK)),
            dma((2, 14)), dma((2, 14)),
        ],
        compiler_params=pltpu.CompilerParams(
            collective_id=0, has_side_effects=True, vmem_limit_bytes=48 << 20
        ),
    )(height, east, north, obs_value, obs_mask, obs_precision, step_sizes)
    return h + inc[0], u + inc[1], v + inc[2]


def solution(mesh):
    spec3 = P(None, "member", "band")
    spec2 = P("member", "band")
    return jax.shard_map(
        per_device,
        mesh=mesh,
        in_specs=(spec3, spec3, spec3, spec2, spec2, spec2, P()),
        out_specs=(spec3, spec3, spec3),
        check_vma=False,
    )
```

```python
import functools
import math

import jax
import jax.numpy as jnp
from jax import lax
from jax.experimental import pallas as pl
from jax.experimental.pallas import tpu as pltpu
from jax.sharding import PartitionSpec as P

MESH = pl.DeviceIdType.MESH
F32 = jnp.float32
BF16 = jnp.bfloat16

MEMBERS = 80
ROWS = 32
COLS = 128
NMEM = 16
NBAND = 8
STEPS = 3
LSCALE = 12.0
REACH = 32
GROUPS = 11
MEAN = 80
CHUNK = 8
NCHUNK = MEMBERS // CHUNK
QUADS = CHUNK // 4
NHALO = MEMBERS // 16
SKEW = 5
TOGETHER = 8
ABOVE, OWN, BELOW = pl.ds(0, 8), pl.ds(8, 32), pl.ds(40, 8)
TOP, BOTTOM = pl.ds(8, 8), pl.ds(32, 8)
CELLS = float(MEMBERS * 512 * 1024)


def taper(offset):
    scaled = offset.astype(F32) / LSCALE
    weight = jnp.exp(-0.5 * scaled * scaled)
    return jnp.where(jnp.abs(offset) <= REACH, weight, 0.0)


def split(x):
    high = x.astype(BF16)
    low = (x - high.astype(F32)).astype(BF16)
    return high, low


def build_tapers(lat_k, lon_k):
    i = lax.broadcasted_iota(jnp.int32, (64, 192), 0)
    j = lax.broadcasted_iota(jnp.int32, (64, 192), 1)
    a = jnp.where(i < 32, i, i - 32)
    jj = jnp.where(j < 96, j, j - 96)
    w = taper(jj - 32 - a)
    high = w.astype(BF16).astype(F32)
    low = jnp.where(j < 96, w - high, 0.0)
    lat_k[...] = jnp.where(i < 32, high, low).astype(BF16)
    k = lax.broadcasted_iota(jnp.int32, (COLS, 2 * COLS), 0)
    n = lax.broadcasted_iota(jnp.int32, (COLS, 2 * COLS), 1)

    def lon(w, n):
        high = w.astype(BF16).astype(F32)
        return jnp.where(n < COLS, high, w - high).astype(BF16)

    out = jnp.where(n < COLS, n, n - COLS)
    own = lon(taper(k - out), n)
    k, n, out = k[:32], n[:32], out[:32]
    left, right = lon(taper(k - 32 - out), n), lon(taper(k + COLS - out), n)
    for s in range(4):
        lon_k[s, pl.ds(0, COLS), :] = own
        lon_k[s, pl.ds(COLS, 2 * COLS), :] = jnp.zeros((2 * COLS, 2 * COLS), BF16)
        lon_k[s, pl.ds(COLS + 32 * s, 32), :] = left
        lon_k[s, pl.ds(2 * COLS + 32 * s, 32), :] = right


def kernel(
    h_in, u_in, v_in, value_in, mask_in, precision_in, steps_in,
    h_out, u_out, v_out, inc,
    x, f, ps, pr, c, rc, lt, ls, lr, g1, lat_k, lon_k, coef, state, s_acc, sq, red,
    obs_value, obs_mask, obs_precision, steps, strip, relay,
    load_sem, store_sem, halo_ss, halo_rs, row_ss, row_rs, relay_rs, col_ss, col_rs, red_ss, red_rs,
):
    m = lax.axis_index("member")
    b = lax.axis_index("band")
    has_up = m > 0
    has_dn = m < NMEM - 1
    up = lax.rem(m + NMEM - 1, NMEM)
    dn = lax.rem(m + 1, NMEM)
    lf = lax.rem(b + NBAND - 1, NBAND)
    rt = lax.rem(b + 1, NBAND)

    core = lax.rem(m, 2)
    y = lax.rem(m // 2, 4)
    z_lo = m // 8
    xx = b // 2
    z = lax.rem(b, 2) * 2 + z_lo

    def at(core_, y_, x_, z_):
        return ((lax.rem(z_, 2) * 4 + y_) * 2 + core_, x_ * 2 + z_ // 2)

    stages = [
        [at(1 - core, y, xx, z)],
        [at(core, lax.rem(y + j, 4), xx, z) for j in (1, 2, 3)],
        [at(core, y, lax.rem(xx + j, 4), z) for j in (1, 2, 3)],
        [at(core, y, xx, lax.rem(z + j, 4)) for j in (1, 2, 3)],
    ]

    near = [(up, b), (dn, b), (m, lf), (m, rt), (up, lf), (up, rt), (dn, lf), (dn, rt)]
    mirror = (z_lo * 8 + 7 - lax.rem(m, 8), b)
    greet = near + [mirror] + [d for stage in stages for d in stage]
    barrier = pltpu.get_barrier_semaphore()
    for d in greet:
        pl.semaphore_signal(barrier, inc=1, device_id=d, device_id_type=MESH)

    loads = [
        pltpu.make_async_copy(src, dst, load_sem.at[k])
        for k, (src, dst) in enumerate((
            (h_in, x.at[0, pl.ds(0, MEMBERS), OWN]),
            (u_in, x.at[1, pl.ds(0, MEMBERS), OWN]),
            (v_in, x.at[2, pl.ds(0, MEMBERS), OWN]),
            (value_in, obs_value),
            (mask_in, obs_mask),
            (precision_in, obs_precision),
            (steps_in, steps),
        ))
    ]
    for copy in loads:
        copy.start()

    lane = lax.broadcasted_iota(jnp.int32, (ROWS, COLS), 1)

    def pack(g, count):
        left = jnp.zeros((ROWS, COLS), F32)
        right = jnp.zeros((ROWS, COLS), F32)
        for s in range(count):
            base = 16 * s
            i = g * 8 + s
            for field, lo, width in ((1, 0, 6), (0, 6, 5), (2, 11, 5)):
                value = x[field, i, OWN]
                where = (lane >= base + lo) & (lane < base + lo + width)
                left = jnp.where(where, pltpu.roll(value, base + lo, 1), left)
                right = jnp.where(where, pltpu.roll(value, (base + lo + width) % COLS, 1), right)
        ps[0, g, OWN] = left
        ps[1, g, OWN] = right

    def halo_copy(k, n, mean=False):
        members = pl.ds(MEAN, 1) if mean else pl.ds(n * 16, 16)
        groups = pl.ds(MEAN // 8, 1) if mean else pl.ds(n * 2, 2)
        src, dst, to = (
            (x.at[:, members, TOP], x.at[:, members, BELOW], (up, b)),
            (ps.at[:, groups, TOP], ps.at[:, groups, BELOW], (up, b)),
            (ps.at[0, groups, TOP], pr.at[1, groups, BELOW], (up, lf)),
            (ps.at[1, groups, TOP], pr.at[0, groups, BELOW], (up, rt)),
            (x.at[:, members, BOTTOM], x.at[:, members, ABOVE], (dn, b)),
            (ps.at[:, groups, BOTTOM], ps.at[:, groups, ABOVE], (dn, b)),
            (ps.at[0, groups, BOTTOM], pr.at[1, groups, ABOVE], (dn, lf)),
            (ps.at[1, groups, BOTTOM], pr.at[0, groups, ABOVE], (dn, rt)),
            (ps.at[0, groups, OWN], pr.at[1, groups, OWN], (m, lf)),
            (ps.at[1, groups, OWN], pr.at[0, groups, OWN], (m, rt)),
        )[k]
        return pltpu.make_async_remote_copy(
            src_ref=src, dst_ref=dst, send_sem=halo_ss.at[n, k], recv_sem=halo_rs.at[n, k],
            device_id=to, device_id_type=MESH,
        )

    def halo_start(n, mean=False):
        for k in (8, 9):
            halo_copy(k, n, mean).start()

        @pl.when(has_up)
        def _():
            for k in range(0, 4):
                halo_copy(k, n, mean).start()

        @pl.when(has_dn)
        def _():
            for k in range(4, 8):
                halo_copy(k, n, mean).start()

    def halo_wait(n, mean=False):
        @pl.when(has_up)
        def _():
            for k in range(4, 8):
                halo_copy(k, n, mean).wait_recv()
            for k in range(0, 4):
                halo_copy(k, n, mean).wait_send()

        @pl.when(has_dn)
        def _():
            for k in range(0, 4):
                halo_copy(k, n, mean).wait_recv()
            for k in range(4, 8):
                halo_copy(k, n, mean).wait_send()

        for k in (8, 9):
            halo_copy(k, n, mean).wait_recv()
            halo_copy(k, n, mean).wait_send()

    def send_halo(n, carry):
        for gg in range(2):
            pack(2 * n + gg, 8)
        halo_start(n)
        return carry

    for copy in loads:
        copy.wait()
    for gg in range(2):
        pack(gg, 8)
    pl.semaphore_wait(barrier, len(greet))
    halo_start(0)

    for k in range(3):
        x[k, MEAN, OWN] = lax.fori_loop(
            0, MEMBERS, lambda i, total, k=k: total + x[k, i, OWN], jnp.zeros((ROWS, COLS), F32), unroll=8
        ) * (1.0 / MEMBERS)
    pack(MEAN // 8, 1)
    halo_start(NHALO, True)

    lax.fori_loop(1, NHALO, send_halo, 0)

    def clear(halo, side):
        x[:, :, halo, :] = jnp.zeros((3, MEMBERS + 8, 8, COLS), F32)
        ps[:, :, halo, :] = jnp.zeros((2, GROUPS, 8, COLS), F32)
        pr[:, :, halo, :] = jnp.zeros((2, GROUPS, 8, COLS), F32)
        for it in range(2):
            rc[it, side] = jnp.zeros((MEMBERS, ROWS, COLS), F32)

    @pl.when(m == 0)
    def _():
        clear(ABOVE, 0)

    @pl.when(m == NMEM - 1)
    def _():
        clear(BELOW, 1)

    build_tapers(lat_k, lon_k)

    tile = lax.broadcasted_iota(jnp.int32, (8, COLS), 0)
    column = lax.broadcasted_iota(jnp.int32, (8, COLS), 1)
    inside = [
        ((6 * tile + j >= 8) | has_up) & ((6 * tile + j < 40) | has_dn) for j in range(6)
    ]
    place = lax.rem(column, 16)
    edge = (column < 6) | (column >= COLS - 6)

    def lon_diff(q):
        return [pltpu.roll(w, COLS - 1, 1) - pltpu.roll(w, 1, 1) for w in q]

    def lat_diff(q):
        out = []
        for first in range(0, len(q), 6):
            part = q[first:first + 6]
            after = part[1:] + [pltpu.roll(part[0], 7, 0)]
            before = [pltpu.roll(part[5], 1, 0)] + part[:5]
            out += [p - w for p, w in zip(after, before)]
        return out

    def advance(hh, uu, vv, keep):
        six = range(len(hh))
        for _ in range(STEPS):
            du, dv = lon_diff(uu), lat_diff(vv)
            hn = [jnp.where(keep[j % 6], hh[j] - 0.2 * (du[j] + dv[j]), 0.0) for j in six]
            dx, dy = lon_diff(hn), lat_diff(hn)
            un = [uu[j] + 0.1 * vv[j] - 0.2 * dx[j] for j in six]
            vn = [jnp.where(inside[j % 6], vv[j] - 0.1 * uu[j] - 0.2 * dy[j], 0.0) for j in six]
            hh, uu, vv = hn, un, vn
        return hh, uu, vv

    def strided(j):
        return pl.ds(j, 8, stride=6)

    def strips(g):
        keep = [w & (place < 12) for w in inside]

        def side(sign, u_shift, h_shift, v_shift, start, u_start):
            far = [pr[sign, g, strided(j)] - ps[1 - sign, g, strided(j)] for j in range(6)]

            def cut(shift, first, width):
                where = (place >= first) & (place < first + width)
                return [jnp.where(where, pltpu.roll(w, shift % COLS, 1) if shift else w, 0.0) for w in far]

            return cut(h_shift, start, 5), cut(u_shift, u_start, 6), cut(v_shift, start, 5)

        left = side(0, 0, -5, -10, 1, 0)
        right = side(1, 6, 0, -5, 6, 6)
        out = advance(*[p + w for p, w in zip(left, right)], keep)
        for k in range(3):
            for j in range(6):
                strip[k, j] = jnp.where(place < 6, out[k][6 + j], out[k][j])

    def forecast(first, s, count):
        out = advance(
            *[[x[k, first + t, strided(j)] for t in range(count) for j in range(6)] for k in range(3)], inside
        )
        for t in range(count):
            shift = (2 * COLS - 6 - 16 * (s + t)) % COLS
            for k in range(3):
                for j in range(6):
                    more = jnp.where(edge, pltpu.roll(strip[k, j], shift, 1), 0.0)
                    f[k, first + t, strided(j)] = out[k][6 * t + j] + more

    halo_wait(NHALO, True)
    strips(MEAN // 8)
    forecast(MEAN, 0, 1)
    mean = [f[k, MEAN, OWN] for k in range(3)]
    for k in range(3):
        state[k] = mean[k]
    obs_weight = obs_mask[...].astype(F32) * obs_precision[...]

    def set_coefficients(sh, su, sv):
        residual = obs_weight * (obs_value[...] - sh - 0.15 * (su * su + sv * sv))
        coef[0] = residual
        coef[1] = 0.3 * su * residual
        coef[2] = 0.3 * sv * residual

    set_coefficients(*mean)

    def row_copy(it, k, n):
        members = pl.ds(n * CHUNK, CHUNK)
        return pltpu.make_async_remote_copy(
            src_ref=c.at[members], dst_ref=rc.at[it, 1 - k, members],
            send_sem=row_ss.at[it, k, n], recv_sem=row_rs.at[it, k, n],
            device_id=near[k], device_id_type=MESH,
        )

    def by_relay(k, n):
        return (m == (8 if k == 0 else 7)) & (lax.rem(n, 2) == 1)

    def at_relay(k, n):
        return (m == (0 if k == 0 else NMEM - 1)) & (lax.rem(n, 2) == 1)

    def relay_in(it, k, n):
        return pltpu.make_async_remote_copy(
            src_ref=c.at[pl.ds(n * CHUNK, CHUNK)], dst_ref=relay.at[it, n // 2],
            send_sem=row_ss.at[it, k, n], recv_sem=relay_rs.at[it, n // 2],
            device_id=(0 if k == 0 else NMEM - 1, b), device_id_type=MESH,
        )

    def relay_out(it, k, n):
        return pltpu.make_async_remote_copy(
            src_ref=relay.at[it, n // 2], dst_ref=rc.at[it, 1 - k, pl.ds(n * CHUNK, CHUNK)],
            send_sem=row_ss.at[it, k, n], recv_sem=row_rs.at[it, k, n],
            device_id=(7 if k == 0 else 8, b), device_id_type=MESH,
        )

    def row_start(it, n):
        for k, there in ((0, has_up), (1, has_dn)):
            pl.when(there & jnp.logical_not(by_relay(k, n)))(row_copy(it, k, n).start)
            pl.when(by_relay(k, n))(relay_in(it, k, n).start)

    def relay_forward(it, n):
        for k in range(2):

            @pl.when(at_relay(k, n))
            def _(k=k):
                relay_in(it, k, n).wait_recv()
                relay_out(it, k, n).start()

    def row_wait(it, n):
        @pl.when(has_up)
        def _():
            row_copy(it, 1, n).wait_recv()

        @pl.when(has_dn)
        def _():
            row_copy(it, 0, n).wait_recv()

    def row_sent(it, n):
        for k, there in ((0, has_up), (1, has_dn)):
            pl.when(there | at_relay(k, n))(row_copy(it, k, n).wait_send)

    def col_copy(it, k, n):
        quads = pl.ds(n * QUADS, QUADS)
        return pltpu.make_async_remote_copy(
            src_ref=ls.at[k, quads], dst_ref=lr.at[it, 1 - k, quads],
            send_sem=col_ss.at[it, k, n], recv_sem=col_rs.at[it, k, n],
            device_id=near[2 + k], device_id_type=MESH,
        )

    scale = 1.0 / math.sqrt(MEMBERS - 1.0)

    def first_chunk(n, carry):
        halo_wait(n)
        for gg in range(2):
            g = n * 2 + gg
            strips(g)

            for s in range(0, 8, TOGETHER):
                first = g * 8 + s
                forecast(first, s, TOGETHER)
                for t in range(TOGETHER):
                    i = first + t
                    total = None
                    for k in range(3):
                        anomaly = (f[k, i, OWN] - state[k]) * scale
                        x[k, i, OWN] = anomaly
                        term = anomaly * coef[k]
                        total = term if total is None else total + term
                    c[i] = total
            row_start(0, g)
        return carry

    lax.fori_loop(0, NHALO, first_chunk, 0)

    stores = [
        pltpu.make_async_copy(f.at[k, pl.ds(0, MEMBERS), OWN], dst, store_sem.at[k])
        for k, dst in enumerate((h_out, u_out, v_out))
    ]
    for copy in stores:
        copy.start()

    def taper_rows(it, n):
        relay_forward(it, n)
        row_wait(it, n)

        for qq in range(QUADS):
            q = n * QUADS + qq
            parts_high, parts_low = [], []
            for ref_part in range(3):
                wide = []
                for s in range(4):
                    i = q * 4 + s
                    wide.append(rc[it, 0, i] if ref_part == 0 else (c[i] if ref_part == 1 else rc[it, 1, i]))
                high, low = split(jnp.concatenate(wide, axis=1))
                parts_high.append(high)
                parts_low.append(low)
            right_side = jnp.concatenate(parts_high + parts_low, axis=0)
            both = jnp.dot(lat_k[...], right_side, preferred_element_type=F32)
            lat = both[:32] + both[32:]
            to_left = jnp.zeros((ROWS, COLS), F32)
            to_right = jnp.zeros((ROWS, COLS), F32)
            for s in range(4):
                part = lat[:, s * COLS:(s + 1) * COLS]
                lt[s, q] = part
                where = (lane >= 32 * s) & (lane < 32 * s + 32)
                to_left = jnp.where(where, pltpu.roll(part, 32 * s, 1) if s else part, to_left)
                to_right = jnp.where(where, pltpu.roll(part, 32 * s + 32, 1) if s < 3 else part, to_right)
            ls[0, q] = to_left
            ls[1, q] = to_right

        for k in range(2):
            col_copy(it, k, n).start()

    def taper_cols(it, n, factor):
        for k in range(2):
            col_copy(it, k, n).wait_recv()
        quads = pl.ds(n * QUADS, QUADS)
        size = QUADS * ROWS
        lh, ll = split(lr[it, 0, quads].reshape(size, COLS))
        rhh, rl = split(lr[it, 1, quads].reshape(size, COLS))
        totals = [None] * 4
        for s in range(4):
            mh, ml = split(lt[s, quads].reshape(size, COLS))
            a = jnp.dot(jnp.concatenate([mh, lh, rhh], axis=1), lon_k[s], preferred_element_type=F32)
            d = jnp.dot(jnp.concatenate([ml, ll, rl], axis=1), lon_k[s, :, pl.ds(0, 128)], preferred_element_type=F32)
            g = (a[:, :COLS] + a[:, COLS:] + d).reshape(QUADS, ROWS, COLS)
            if it == 0:
                g1[s, quads] = g
            else:
                g = factor * g1[s, quads] - g
            for qq in range(QUADS):
                i = (n * QUADS + qq) * 4 + s
                part = g[qq]
                terms = [x[k, i, OWN] * part for k in range(3)] + [part * part]
                totals = [t if o is None else o + t for o, t in zip(totals, terms)]
        for k in range(3):
            s_acc[it, k] += totals[k]
        sq[...] += totals[3]

    def localize(it, factor):
        def body(n, carry):
            @pl.when(n < NCHUNK)
            def _():
                taper_rows(it, n)

            @pl.when(n >= SKEW)
            def _():
                taper_cols(it, n - SKEW, factor)

            return carry

        lax.fori_loop(0, NCHUNK + SKEW, body, 0)

    def sum_all(it):
        value = sq[...]
        value = value[:8] + value[8:16] + value[16:24] + value[24:]
        slot = 0
        for stage in stages:
            red[it, slot] = value
            copies = [
                pltpu.make_async_remote_copy(
                    src_ref=red.at[it, slot], dst_ref=red.at[it, slot + 1 + j],
                    send_sem=red_ss.at[it, slot + j], recv_sem=red_rs.at[it, slot + j],
                    device_id=d, device_id_type=MESH,
                )
                for j, d in enumerate(stage)
            ]
            for copy in copies:
                copy.start()
            for copy in copies:
                copy.wait_recv()
            for j in range(len(stage)):
                value = value + red[it, slot + 1 + j]
            for copy in copies:
                copy.wait_send()
            slot += 1 + len(stage)
        total = jnp.sum(jnp.sum(value, axis=0, keepdims=True), axis=1, keepdims=True)
        return steps[it].astype(F32) / 64.0 / jnp.sqrt(total / CELLS + 1e-6)

    for it in range(2):
        for k in range(3):
            s_acc[it, k] = jnp.zeros((ROWS, COLS), F32)
    sq[...] = jnp.zeros((ROWS, COLS), F32)
    localize(0, None)
    factor1 = sum_all(0)

    def sent(n, carry):
        row_sent(0, n)
        for k in range(2):
            col_copy(0, k, n).wait_send()
        return carry

    lax.fori_loop(0, NCHUNK, sent, 0)
    sq[...] = jnp.zeros((ROWS, COLS), F32)
    set_coefficients(*[state[k] + factor1 * s_acc[0, k] for k in range(3)])

    def second_chunk(n, carry):
        def one(j, carry2):
            i = n * CHUNK + j
            c[i] = x[0, i, OWN] * coef[0] + x[1, i, OWN] * coef[1] + x[2, i, OWN] * coef[2]
            return carry2

        lax.fori_loop(0, CHUNK, one, 0, unroll=4)
        row_start(1, n)
        return carry

    lax.fori_loop(0, NCHUNK, second_chunk, 0)
    localize(1, factor1)
    factor2 = sum_all(1)
    for k in range(3):
        inc[k] = factor1 * s_acc[0, k] - factor2 * s_acc[1, k]

    def sent2(n, carry):
        row_sent(1, n)
        for k in range(2):
            col_copy(1, k, n).wait_send()
        return carry

    lax.fori_loop(0, NCHUNK, sent2, 0)
    for copy in stores:
        copy.wait()


def per_device(height, east, north, obs_value, obs_mask, obs_precision, step_sizes):
    block = (MEMBERS, ROWS, COLS)
    vmem = pl.BlockSpec(memory_space=pltpu.VMEM)
    anyspace = pl.BlockSpec(memory_space=pl.ANY)
    dma = pltpu.SemaphoreType.DMA
    h, u, v, inc = pl.pallas_call(
        kernel,
        name="analysis",
        out_shape=[jax.ShapeDtypeStruct(block, F32)] * 3 + [jax.ShapeDtypeStruct((3, ROWS, COLS), F32)],
        in_specs=[pl.BlockSpec(memory_space=pltpu.HBM)] * 7,
        out_specs=[anyspace] * 3 + [vmem],
        scratch_shapes=[
            pltpu.VMEM((3, MEMBERS + 8, 48, COLS), F32),
            pltpu.VMEM((3, MEMBERS + 1, 48, COLS), F32),
            pltpu.VMEM((2, GROUPS, 48, COLS), F32),
            pltpu.VMEM((2, GROUPS, 48, COLS), F32),
            pltpu.VMEM(block, F32),
            pltpu.VMEM((2, 2) + block, F32),
            pltpu.VMEM((4, MEMBERS // 4, ROWS, COLS), F32),
            pltpu.VMEM((2, MEMBERS // 4, ROWS, COLS), F32),
            pltpu.VMEM((2, 2, MEMBERS // 4, ROWS, COLS), F32),
            pltpu.VMEM((4, MEMBERS // 4, ROWS, COLS), F32),
            pltpu.VMEM((64, 192), BF16),
            pltpu.VMEM((4, 384, 256), BF16),
            pltpu.VMEM((3, ROWS, COLS), F32),
            pltpu.VMEM((3, ROWS, COLS), F32),
            pltpu.VMEM((2, 3, ROWS, COLS), F32),
            pltpu.VMEM((ROWS, COLS), F32),
            pltpu.VMEM((2, 14, 8, COLS), F32),
            pltpu.VMEM((ROWS, COLS), F32),
            pltpu.VMEM((ROWS, COLS), jnp.int32),
            pltpu.VMEM((ROWS, COLS), F32),
            pltpu.SMEM((2,), jnp.int32),
            pltpu.VMEM((3, 6, 8, COLS), F32),
            pltpu.VMEM((2, NCHUNK // 2, CHUNK, ROWS, COLS), F32),
            dma((7,)), dma((3,)),
            dma((NHALO + 1, 10)), dma((NHALO + 1, 10)),
            dma((2, 2, NCHUNK)), dma((2, 2, NCHUNK)), dma((2, NCHUNK // 2)),
            dma((2, 2, NCHUNK)), dma((2, 2, NCHUNK)),
            dma((2, 14)), dma((2, 14)),
        ],
        compiler_params=pltpu.CompilerParams(
            collective_id=0, has_side_effects=True, vmem_limit_bytes=48 << 20
        ),
    )(height, east, north, obs_value, obs_mask, obs_precision, step_sizes)
    return h + inc[0], u + inc[1], v + inc[2]


def solution(mesh):
    spec3 = P(None, "member", "band")
    spec2 = P("member", "band")
    return jax.shard_map(
        per_device,
        mesh=mesh,
        in_specs=(spec3, spec3, spec3, spec2, spec2, spec2, P()),
        out_specs=(spec3, spec3, spec3),
        check_vma=False,
    )
```

```python
import functools
import math

import jax
import jax.numpy as jnp
from jax import lax
from jax.experimental import pallas as pl
from jax.experimental.pallas import tpu as pltpu
from jax.sharding import PartitionSpec as P

MESH = pl.DeviceIdType.MESH
F32 = jnp.float32
BF16 = jnp.bfloat16

MEMBERS = 80
ROWS = 32
COLS = 128
NMEM = 16
NBAND = 8
STEPS = 3
LSCALE = 12.0
REACH = 32
GROUPS = 11
MEAN = 80
CHUNK = 8
NCHUNK = MEMBERS // CHUNK
QUADS = CHUNK // 4
NHALO = MEMBERS // 16
SKEW = 5
TOGETHER = 8
ABOVE, OWN, BELOW = pl.ds(0, 8), pl.ds(8, 32), pl.ds(40, 8)
TOP, BOTTOM = pl.ds(8, 8), pl.ds(32, 8)
CELLS = float(MEMBERS * 512 * 1024)


def taper(offset):
    scaled = offset.astype(F32) / LSCALE
    weight = jnp.exp(-0.5 * scaled * scaled)
    return jnp.where(jnp.abs(offset) <= REACH, weight, 0.0)


def split(x):
    high = x.astype(BF16)
    low = (x - high.astype(F32)).astype(BF16)
    return high, low


def build_tapers(lat_k, lon_k):
    i = lax.broadcasted_iota(jnp.int32, (64, 192), 0)
    j = lax.broadcasted_iota(jnp.int32, (64, 192), 1)
    a = jnp.where(i < 32, i, i - 32)
    jj = jnp.where(j < 96, j, j - 96)
    w = taper(jj - 32 - a)
    high = w.astype(BF16).astype(F32)
    low = jnp.where(j < 96, w - high, 0.0)
    lat_k[...] = jnp.where(i < 32, high, low).astype(BF16)
    k = lax.broadcasted_iota(jnp.int32, (COLS, 2 * COLS), 0)
    n = lax.broadcasted_iota(jnp.int32, (COLS, 2 * COLS), 1)

    def lon(w, n):
        high = w.astype(BF16).astype(F32)
        return jnp.where(n < COLS, high, w - high).astype(BF16)

    out = jnp.where(n < COLS, n, n - COLS)
    own = lon(taper(k - out), n)
    k, n, out = k[:32], n[:32], out[:32]
    left, right = lon(taper(k - 32 - out), n), lon(taper(k + COLS - out), n)
    for s in range(4):
        lon_k[s, pl.ds(0, COLS), :] = own
        lon_k[s, pl.ds(COLS, 2 * COLS), :] = jnp.zeros((2 * COLS, 2 * COLS), BF16)
        lon_k[s, pl.ds(COLS + 32 * s, 32), :] = left
        lon_k[s, pl.ds(2 * COLS + 32 * s, 32), :] = right


def kernel(
    h_in, u_in, v_in, observed_in,
    h_out, u_out, v_out, inc,
    x, f, ps, pr, c, rc, lt, ls, lr, g1, lat_k, lon_k, coef, state, s_acc, sq, red,
    observed, strip, relay, relay_x, relay_p,
    load_sem, store_sem, halo_ss, halo_rs, halo_relay_rs, row_ss, row_rs, relay_rs, col_ss, col_rs, red_ss, red_rs,
):
    m = lax.axis_index("member")
    b = lax.axis_index("band")
    has_up = m > 0
    has_dn = m < NMEM - 1
    up = lax.rem(m + NMEM - 1, NMEM)
    dn = lax.rem(m + 1, NMEM)
    lf = lax.rem(b + NBAND - 1, NBAND)
    rt = lax.rem(b + 1, NBAND)

    core = lax.rem(m, 2)
    y = lax.rem(m // 2, 4)
    z_lo = m // 8
    xx = b // 2
    z = lax.rem(b, 2) * 2 + z_lo

    def at(core_, y_, x_, z_):
        return ((lax.rem(z_, 2) * 4 + y_) * 2 + core_, x_ * 2 + z_ // 2)

    stages = [
        [at(1 - core, y, xx, z)],
        [at(core, lax.rem(y + j, 4), xx, z) for j in (1, 2, 3)],
        [at(core, y, lax.rem(xx + j, 4), z) for j in (1, 2, 3)],
        [at(core, y, xx, lax.rem(z + j, 4)) for j in (1, 2, 3)],
    ]

    near = [(up, b), (dn, b), (m, lf), (m, rt), (up, lf), (up, rt), (dn, lf), (dn, rt)]
    mirror = (z_lo * 8 + 7 - lax.rem(m, 8), b)
    greet = near + [mirror] + [d for stage in stages for d in stage]
    barrier = pltpu.get_barrier_semaphore()
    for d in greet:
        pl.semaphore_signal(barrier, inc=1, device_id=d, device_id_type=MESH)

    loads = [
        pltpu.make_async_copy(src, dst, load_sem.at[k])
        for k, (src, dst) in enumerate((
            (h_in, x.at[0, pl.ds(0, MEMBERS), OWN]),
            (u_in, x.at[1, pl.ds(0, MEMBERS), OWN]),
            (v_in, x.at[2, pl.ds(0, MEMBERS), OWN]),
            (observed_in, observed),
        ))
    ]
    for copy in loads:
        copy.start()

    lane = lax.broadcasted_iota(jnp.int32, (ROWS, COLS), 1)

    def pack(g, count):
        left = jnp.zeros((ROWS, COLS), F32)
        right = jnp.zeros((ROWS, COLS), F32)
        for s in range(count):
            base = 16 * s
            i = g * 8 + s
            for field, lo, width in ((1, 0, 6), (0, 6, 5), (2, 11, 5)):
                value = x[field, i, OWN]
                where = (lane >= base + lo) & (lane < base + lo + width)
                left = jnp.where(where, pltpu.roll(value, base + lo, 1), left)
                right = jnp.where(where, pltpu.roll(value, (base + lo + width) % COLS, 1), right)
        ps[0, g, OWN] = left
        ps[1, g, OWN] = right

    def halo_copy(k, n, mean=False):
        members = pl.ds(MEAN, 1) if mean else pl.ds(n * 16, 16)
        groups = pl.ds(MEAN // 8, 1) if mean else pl.ds(n * 2, 2)
        src, dst, to = (
            (x.at[:, members, TOP], x.at[:, members, BELOW], (up, b)),
            (ps.at[:, groups, TOP], ps.at[:, groups, BELOW], (up, b)),
            (ps.at[0, groups, TOP], pr.at[1, groups, BELOW], (up, lf)),
            (ps.at[1, groups, TOP], pr.at[0, groups, BELOW], (up, rt)),
            (x.at[:, members, BOTTOM], x.at[:, members, ABOVE], (dn, b)),
            (ps.at[:, groups, BOTTOM], ps.at[:, groups, ABOVE], (dn, b)),
            (ps.at[0, groups, BOTTOM], pr.at[1, groups, ABOVE], (dn, lf)),
            (ps.at[1, groups, BOTTOM], pr.at[0, groups, ABOVE], (dn, rt)),
            (ps.at[0, groups, OWN], pr.at[1, groups, OWN], (m, lf)),
            (ps.at[1, groups, OWN], pr.at[0, groups, OWN], (m, rt)),
        )[k]
        return pltpu.make_async_remote_copy(
            src_ref=src, dst_ref=dst, send_sem=halo_ss.at[n, k], recv_sem=halo_rs.at[n, k],
            device_id=to, device_id_type=MESH,
        )

    def halo_relay_in(k, n):
        part = k % 4
        return pltpu.make_async_remote_copy(
            src_ref=(x.at[:, pl.ds(n * 16, 16), TOP if k < 4 else BOTTOM] if part == 0
                     else ps.at[:, pl.ds(n * 2, 2), TOP if k < 4 else BOTTOM]),
            dst_ref=(relay_x if part == 0 else relay_p).at[n // 2],
            send_sem=halo_ss.at[n, k], recv_sem=halo_relay_rs.at[n // 2, part],
            device_id=(0 if k < 4 else NMEM - 1, b), device_id_type=MESH,
        )

    def halo_relay_out(k, n):
        part = k % 4
        rows = BELOW if k < 4 else ABOVE
        return pltpu.make_async_remote_copy(
            src_ref=(relay_x if part == 0 else relay_p).at[n // 2],
            dst_ref=x.at[:, pl.ds(n * 16, 16), rows] if part == 0 else ps.at[:, pl.ds(n * 2, 2), rows],
            send_sem=halo_ss.at[n, k], recv_sem=halo_rs.at[n, k],
            device_id=(7 if k < 4 else 8, b), device_id_type=MESH,
        )

    def halo_forward(n):
        for end, ks in ((0, (0, 1)), (NMEM - 1, (4, 5))):

            @pl.when((m == end) & (lax.rem(n, 2) == 1))
            def _(ks=ks):
                for k in ks:
                    halo_relay_in(k, n).wait_recv()
                    halo_relay_out(k, n).start()

    def halo_start(n, mean=False):
        for k in (8, 9):
            halo_copy(k, n, mean).start()
        odd = False if mean else lax.rem(n, 2) == 1
        for there, source, ks in ((has_up, 8, range(0, 4)), (has_dn, 7, range(4, 8))):
            away = (m == source) & odd

            @pl.when(there & jnp.logical_not(away))
            def _(ks=ks):
                for k in ks[:2]:
                    halo_copy(k, n, mean).start()

            if not mean:

                @pl.when(away)
                def _(ks=ks):
                    for k in ks[:2]:
                        halo_relay_in(k, n).start()

            @pl.when(there)
            def _(ks=ks):
                for k in ks[2:]:
                    halo_copy(k, n, mean).start()

    def halo_wait(n, mean=False):
        @pl.when(has_up)
        def _():
            for k in range(4, 8):
                halo_copy(k, n, mean).wait_recv()
            for k in range(0, 4):
                halo_copy(k, n, mean).wait_send()

        @pl.when(has_dn)
        def _():
            for k in range(0, 4):
                halo_copy(k, n, mean).wait_recv()
            for k in range(4, 8):
                halo_copy(k, n, mean).wait_send()

        for k in (8, 9):
            halo_copy(k, n, mean).wait_recv()
            halo_copy(k, n, mean).wait_send()

        if not mean:
            for end, ks in ((0, (0, 1)), (NMEM - 1, (4, 5))):

                @pl.when((m == end) & (lax.rem(n, 2) == 1))
                def _(ks=ks):
                    for k in ks:
                        halo_relay_out(k, n).wait_send()

    def send_halo(n, carry):
        for gg in range(2):
            pack(2 * n + gg, 8)
        halo_start(n)
        return carry

    for copy in loads:
        copy.wait()
    for gg in range(2):
        pack(gg, 8)
    pl.semaphore_wait(barrier, len(greet))
    halo_start(0)

    for k in range(3):
        x[k, MEAN, OWN] = lax.fori_loop(
            0, MEMBERS, lambda i, total, k=k: total + x[k, i, OWN], jnp.zeros((ROWS, COLS), F32), unroll=8
        ) * (1.0 / MEMBERS)
    pack(MEAN // 8, 1)
    halo_start(NHALO, True)

    lax.fori_loop(1, NHALO, send_halo, 0)

    def clear(halo, side):
        x[:, :, halo, :] = jnp.zeros((3, MEMBERS + 8, 8, COLS), F32)
        ps[:, :, halo, :] = jnp.zeros((2, GROUPS, 8, COLS), F32)
        pr[:, :, halo, :] = jnp.zeros((2, GROUPS, 8, COLS), F32)
        for it in range(2):
            rc[it, side] = jnp.zeros((MEMBERS, ROWS, COLS), F32)

    @pl.when(m == 0)
    def _():
        clear(ABOVE, 0)

    @pl.when(m == NMEM - 1)
    def _():
        clear(BELOW, 1)

    build_tapers(lat_k, lon_k)

    tile = lax.broadcasted_iota(jnp.int32, (8, COLS), 0)
    column = lax.broadcasted_iota(jnp.int32, (8, COLS), 1)
    inside = [
        ((6 * tile + j >= 8) | has_up) & ((6 * tile + j < 40) | has_dn) for j in range(6)
    ]
    place = lax.rem(column, 16)
    edge = (column < 6) | (column >= COLS - 6)

    def lon_diff(q):
        return [pltpu.roll(w, COLS - 1, 1) - pltpu.roll(w, 1, 1) for w in q]

    def lat_diff(q):
        out = []
        for first in range(0, len(q), 6):
            part = q[first:first + 6]
            after = part[1:] + [pltpu.roll(part[0], 7, 0)]
            before = [pltpu.roll(part[5], 1, 0)] + part[:5]
            out += [p - w for p, w in zip(after, before)]
        return out

    def advance(hh, uu, vv, keep):
        six = range(len(hh))
        for _ in range(STEPS):
            du, dv = lon_diff(uu), lat_diff(vv)
            hn = [jnp.where(keep[j % 6], hh[j] - 0.2 * (du[j] + dv[j]), 0.0) for j in six]
            dx, dy = lon_diff(hn), lat_diff(hn)
            un = [uu[j] + 0.1 * vv[j] - 0.2 * dx[j] for j in six]
            vn = [jnp.where(inside[j % 6], vv[j] - 0.1 * uu[j] - 0.2 * dy[j], 0.0) for j in six]
            hh, uu, vv = hn, un, vn
        return hh, uu, vv

    def strided(j):
        return pl.ds(j, 8, stride=6)

    def strips(g):
        keep = [w & (place < 12) for w in inside]

        def side(sign, u_shift, h_shift, v_shift, start, u_start):
            far = [pr[sign, g, strided(j)] - ps[1 - sign, g, strided(j)] for j in range(6)]

            def cut(shift, first, width):
                where = (place >= first) & (place < first + width)
                return [jnp.where(where, pltpu.roll(w, shift % COLS, 1) if shift else w, 0.0) for w in far]

            return cut(h_shift, start, 5), cut(u_shift, u_start, 6), cut(v_shift, start, 5)

        left = side(0, 0, -5, -10, 1, 0)
        right = side(1, 6, 0, -5, 6, 6)
        out = advance(*[p + w for p, w in zip(left, right)], keep)
        for k in range(3):
            for j in range(6):
                strip[k, j] = jnp.where(place < 6, out[k][6 + j], out[k][j])

    def forecast(first, s, count):
        out = advance(
            *[[x[k, first + t, strided(j)] for t in range(count) for j in range(6)] for k in range(3)], inside
        )
        for t in range(count):
            shift = (2 * COLS - 6 - 16 * (s + t)) % COLS
            for k in range(3):
                for j in range(6):
                    more = jnp.where(edge, pltpu.roll(strip[k, j], shift, 1), 0.0)
                    f[k, first + t, strided(j)] = out[k][6 * t + j] + more

    halo_wait(NHALO, True)
    strips(MEAN // 8)
    forecast(MEAN, 0, 1)
    mean = [f[k, MEAN, OWN] for k in range(3)]
    for k in range(3):
        state[k] = mean[k]

    def set_coefficients(sh, su, sv):
        residual = observed[pl.ds(ROWS, ROWS)] * (observed[pl.ds(0, ROWS)] - sh - 0.15 * (su * su + sv * sv))
        coef[0] = residual
        coef[1] = 0.3 * su * residual
        coef[2] = 0.3 * sv * residual

    set_coefficients(*mean)

    def row_copy(it, k, n):
        members = pl.ds(n * CHUNK, CHUNK)
        return pltpu.make_async_remote_copy(
            src_ref=c.at[members], dst_ref=rc.at[it, 1 - k, members],
            send_sem=row_ss.at[it, k, n], recv_sem=row_rs.at[it, k, n],
            device_id=near[k], device_id_type=MESH,
        )

    def by_relay(k, n):
        return (m == (8 if k == 0 else 7)) & (lax.rem(n, 2) == 1)

    def at_relay(k, n):
        return (m == (0 if k == 0 else NMEM - 1)) & (lax.rem(n, 2) == 1)

    def relay_in(it, k, n):
        return pltpu.make_async_remote_copy(
            src_ref=c.at[pl.ds(n * CHUNK, CHUNK)], dst_ref=relay.at[it, n // 2],
            send_sem=row_ss.at[it, k, n], recv_sem=relay_rs.at[it, n // 2],
            device_id=(0 if k == 0 else NMEM - 1, b), device_id_type=MESH,
        )

    def relay_out(it, k, n):
        return pltpu.make_async_remote_copy(
            src_ref=relay.at[it, n // 2], dst_ref=rc.at[it, 1 - k, pl.ds(n * CHUNK, CHUNK)],
            send_sem=row_ss.at[it, k, n], recv_sem=row_rs.at[it, k, n],
            device_id=(7 if k == 0 else 8, b), device_id_type=MESH,
        )

    def row_start(it, n):
        for k, there in ((0, has_up), (1, has_dn)):
            pl.when(there & jnp.logical_not(by_relay(k, n)))(row_copy(it, k, n).start)
            pl.when(by_relay(k, n))(relay_in(it, k, n).start)

    def relay_forward(it, n):
        for k in range(2):

            @pl.when(at_relay(k, n))
            def _(k=k):
                relay_in(it, k, n).wait_recv()
                relay_out(it, k, n).start()

    def row_wait(it, n):
        @pl.when(has_up)
        def _():
            row_copy(it, 1, n).wait_recv()

        @pl.when(has_dn)
        def _():
            row_copy(it, 0, n).wait_recv()

    def row_sent(it, n):
        for k, there in ((0, has_up), (1, has_dn)):
            pl.when(there | at_relay(k, n))(row_copy(it, k, n).wait_send)

    def col_copy(it, k, n):
        quads = pl.ds(n * QUADS, QUADS)
        return pltpu.make_async_remote_copy(
            src_ref=ls.at[k, quads], dst_ref=lr.at[it, 1 - k, quads],
            send_sem=col_ss.at[it, k, n], recv_sem=col_rs.at[it, k, n],
            device_id=near[2 + k], device_id_type=MESH,
        )

    scale = 1.0 / math.sqrt(MEMBERS - 1.0)

    def first_chunk(n, carry):
        halo_wait(n)
        pl.when(n + 1 < NHALO)(lambda: halo_forward(n + 1))
        for gg in range(2):
            g = n * 2 + gg
            strips(g)

            for s in range(0, 8, TOGETHER):
                first = g * 8 + s
                forecast(first, s, TOGETHER)
                for t in range(TOGETHER):
                    i = first + t
                    total = None
                    for k in range(3):
                        anomaly = (f[k, i, OWN] - state[k]) * scale
                        x[k, i, OWN] = anomaly
                        term = anomaly * coef[k]
                        total = term if total is None else total + term
                    c[i] = total
            row_start(0, g)
        return carry

    lax.fori_loop(0, NHALO, first_chunk, 0)

    stores = [
        pltpu.make_async_copy(f.at[k, pl.ds(0, MEMBERS), OWN], dst, store_sem.at[k])
        for k, dst in enumerate((h_out, u_out, v_out))
    ]
    for copy in stores:
        copy.start()

    def taper_rows(it, n):
        relay_forward(it, n)
        row_wait(it, n)

        for qq in range(QUADS):
            q = n * QUADS + qq
            parts_high, parts_low = [], []
            for ref_part in range(3):
                wide = []
                for s in range(4):
                    i = q * 4 + s
                    wide.append(rc[it, 0, i] if ref_part == 0 else (c[i] if ref_part == 1 else rc[it, 1, i]))
                high, low = split(jnp.concatenate(wide, axis=1))
                parts_high.append(high)
                parts_low.append(low)
            right_side = jnp.concatenate(parts_high + parts_low, axis=0)
            both = jnp.dot(lat_k[...], right_side, preferred_element_type=F32)
            lat = both[:32] + both[32:]
            to_left = jnp.zeros((ROWS, COLS), F32)
            to_right = jnp.zeros((ROWS, COLS), F32)
            for s in range(4):
                part = lat[:, s * COLS:(s + 1) * COLS]
                lt[s, q] = part
                where = (lane >= 32 * s) & (lane < 32 * s + 32)
                to_left = jnp.where(where, pltpu.roll(part, 32 * s, 1) if s else part, to_left)
                to_right = jnp.where(where, pltpu.roll(part, 32 * s + 32, 1) if s < 3 else part, to_right)
            ls[0, q] = to_left
            ls[1, q] = to_right

        for k in range(2):
            col_copy(it, k, n).start()

    def taper_cols(it, n, factor):
        for k in range(2):
            col_copy(it, k, n).wait_recv()
        quads = pl.ds(n * QUADS, QUADS)
        size = QUADS * ROWS
        lh, ll = split(lr[it, 0, quads].reshape(size, COLS))
        rhh, rl = split(lr[it, 1, quads].reshape(size, COLS))
        totals = [None] * 4
        for s in range(4):
            mh, ml = split(lt[s, quads].reshape(size, COLS))
            a = jnp.dot(jnp.concatenate([mh, lh, rhh], axis=1), lon_k[s], preferred_element_type=F32)
            d = jnp.dot(jnp.concatenate([ml, ll, rl], axis=1), lon_k[s, :, pl.ds(0, 128)], preferred_element_type=F32)
            g = (a[:, :COLS] + a[:, COLS:] + d).reshape(QUADS, ROWS, COLS)
            if it == 0:
                g1[s, quads] = g
            else:
                g = factor * g1[s, quads] - g
            for qq in range(QUADS):
                i = (n * QUADS + qq) * 4 + s
                part = g[qq]
                terms = [x[k, i, OWN] * part for k in range(3)] + [part * part]
                totals = [t if o is None else o + t for o, t in zip(totals, terms)]
        for k in range(3):
            s_acc[it, k] += totals[k]
        sq[...] += totals[3]

    def localize(it, factor):
        def body(n, carry):
            @pl.when(n < NCHUNK)
            def _():
                taper_rows(it, n)

            @pl.when(n >= SKEW)
            def _():
                taper_cols(it, n - SKEW, factor)

            return carry

        lax.fori_loop(0, NCHUNK + SKEW, body, 0)

    def sum_all(it):
        value = sq[...]
        value = value[:8] + value[8:16] + value[16:24] + value[24:]
        slot = 0
        for stage in stages:
            red[it, slot] = value
            copies = [
                pltpu.make_async_remote_copy(
                    src_ref=red.at[it, slot], dst_ref=red.at[it, slot + 1 + j],
                    send_sem=red_ss.at[it, slot + j], recv_sem=red_rs.at[it, slot + j],
                    device_id=d, device_id_type=MESH,
                )
                for j, d in enumerate(stage)
            ]
            for copy in copies:
                copy.start()
            for copy in copies:
                copy.wait_recv()
            for j in range(len(stage)):
                value = value + red[it, slot + 1 + j]
            for copy in copies:
                copy.wait_send()
            slot += 1 + len(stage)
        total = jnp.sum(jnp.sum(value, axis=0, keepdims=True), axis=1, keepdims=True)
        return observed[pl.ds(2 * ROWS + 8 * it, 1), pl.ds(0, 1)] / jnp.sqrt(total / CELLS + 1e-6)

    for it in range(2):
        for k in range(3):
            s_acc[it, k] = jnp.zeros((ROWS, COLS), F32)
    sq[...] = jnp.zeros((ROWS, COLS), F32)
    localize(0, None)
    factor1 = sum_all(0)

    def sent(n, carry):
        row_sent(0, n)
        for k in range(2):
            col_copy(0, k, n).wait_send()
        return carry

    lax.fori_loop(0, NCHUNK, sent, 0)
    sq[...] = jnp.zeros((ROWS, COLS), F32)
    set_coefficients(*[state[k] + factor1 * s_acc[0, k] for k in range(3)])

    def second_chunk(n, carry):
        def one(j, carry2):
            i = n * CHUNK + j
            c[i] = x[0, i, OWN] * coef[0] + x[1, i, OWN] * coef[1] + x[2, i, OWN] * coef[2]
            return carry2

        lax.fori_loop(0, CHUNK, one, 0, unroll=4)
        row_start(1, n)
        return carry

    lax.fori_loop(0, NCHUNK, second_chunk, 0)
    localize(1, factor1)
    factor2 = sum_all(1)
    for k in range(3):
        inc[k] = factor1 * s_acc[0, k] - factor2 * s_acc[1, k]

    def sent2(n, carry):
        row_sent(1, n)
        for k in range(2):
            col_copy(1, k, n).wait_send()
        return carry

    lax.fori_loop(0, NCHUNK, sent2, 0)
    for copy in stores:
        copy.wait()


def per_device(height, east, north, obs_value, obs_mask, obs_precision, step_sizes):
    block = (MEMBERS, ROWS, COLS)
    vmem = pl.BlockSpec(memory_space=pltpu.VMEM)
    anyspace = pl.BlockSpec(memory_space=pl.ANY)
    dma = pltpu.SemaphoreType.DMA
    steps = jnp.broadcast_to((step_sizes.astype(F32) / 64.0)[:, None, None], (2, 8, COLS))
    observed = jnp.concatenate(
        [obs_value, obs_mask.astype(F32) * obs_precision, steps.reshape(16, COLS)], axis=0
    )
    h, u, v, inc = pl.pallas_call(
        kernel,
        name="analysis",
        out_shape=[jax.ShapeDtypeStruct(block, F32)] * 3 + [jax.ShapeDtypeStruct((3, ROWS, COLS), F32)],
        in_specs=[pl.BlockSpec(memory_space=pltpu.HBM)] * 4,
        out_specs=[anyspace] * 3 + [vmem],
        scratch_shapes=[
            pltpu.VMEM((3, MEMBERS + 8, 48, COLS), F32),
            pltpu.VMEM((3, MEMBERS + 1, 48, COLS), F32),
            pltpu.VMEM((2, GROUPS, 48, COLS), F32),
            pltpu.VMEM((2, GROUPS, 48, COLS), F32),
            pltpu.VMEM(block, F32),
            pltpu.VMEM((2, 2) + block, F32),
            pltpu.VMEM((4, MEMBERS // 4, ROWS, COLS), F32),
            pltpu.VMEM((2, MEMBERS // 4, ROWS, COLS), F32),
            pltpu.VMEM((2, 2, MEMBERS // 4, ROWS, COLS), F32),
            pltpu.VMEM((4, MEMBERS // 4, ROWS, COLS), F32),
            pltpu.VMEM((64, 192), BF16),
            pltpu.VMEM((4, 384, 256), BF16),
            pltpu.VMEM((3, ROWS, COLS), F32),
            pltpu.VMEM((3, ROWS, COLS), F32),
            pltpu.VMEM((2, 3, ROWS, COLS), F32),
            pltpu.VMEM((ROWS, COLS), F32),
            pltpu.VMEM((2, 14, 8, COLS), F32),
            pltpu.VMEM((2 * ROWS + 16, COLS), F32),
            pltpu.VMEM((3, 6, 8, COLS), F32),
            pltpu.VMEM((2, NCHUNK // 2, CHUNK, ROWS, COLS), F32),
            pltpu.VMEM((NHALO // 2, 3, 16, 8, COLS), F32),
            pltpu.VMEM((NHALO // 2, 2, 2, 8, COLS), F32),
            dma((4,)), dma((3,)),
            dma((NHALO + 1, 10)), dma((NHALO + 1, 10)), dma((NHALO // 2, 2)),
            dma((2, 2, NCHUNK)), dma((2, 2, NCHUNK)), dma((2, NCHUNK // 2)),
            dma((2, 2, NCHUNK)), dma((2, 2, NCHUNK)),
            dma((2, 14)), dma((2, 14)),
        ],
        compiler_params=pltpu.CompilerParams(
            collective_id=0, has_side_effects=True, vmem_limit_bytes=50 << 20
        ),
    )(height, east, north, observed)
    return h + inc[0], u + inc[1], v + inc[2]


def solution(mesh):
    spec3 = P(None, "member", "band")
    spec2 = P("member", "band")
    return jax.shard_map(
        per_device,
        mesh=mesh,
        in_specs=(spec3, spec3, spec3, spec2, spec2, spec2, P()),
        out_specs=(spec3, spec3, spec3),
        check_vma=False,
    )
```

```python
import functools
import math

import jax
import jax.numpy as jnp
from jax import lax
from jax.experimental import pallas as pl
from jax.experimental.pallas import tpu as pltpu
from jax.sharding import PartitionSpec as P

MESH = pl.DeviceIdType.MESH
F32 = jnp.float32
BF16 = jnp.bfloat16

MEMBERS = 80
ROWS = 32
COLS = 128
NMEM = 16
NBAND = 8
STEPS = 3
LSCALE = 12.0
REACH = 32
GROUPS = 11
MEAN = 80
CHUNK = 8
NCHUNK = MEMBERS // CHUNK
QUADS = CHUNK // 4
NHALO = MEMBERS // 16
SKEW = 5
LAG = 3
BEHIND = 5
TOGETHER = 8
ABOVE, OWN, BELOW = pl.ds(2, 6), pl.ds(8, 32), pl.ds(40, 6)
TOP, BOTTOM = pl.ds(8, 6), pl.ds(34, 6)
CELLS = float(MEMBERS * 512 * 1024)


def taper(offset):
    scaled = offset.astype(F32) / LSCALE
    weight = jnp.exp(-0.5 * scaled * scaled)
    return jnp.where(jnp.abs(offset) <= REACH, weight, 0.0)


def split(x):
    high = x.astype(BF16)
    low = (x - high.astype(F32)).astype(BF16)
    return high, low


def build_tapers(lat_k, lon_k):
    i = lax.broadcasted_iota(jnp.int32, (64, 192), 0)
    j = lax.broadcasted_iota(jnp.int32, (64, 192), 1)
    a = jnp.where(i < 32, i, i - 32)
    jj = jnp.where(j < 96, j, j - 96)
    w = taper(jj - 32 - a)
    high = w.astype(BF16).astype(F32)
    low = jnp.where(j < 96, w - high, 0.0)
    lat_k[...] = jnp.where(i < 32, high, low).astype(BF16)
    k = lax.broadcasted_iota(jnp.int32, (COLS, 2 * COLS), 0)
    n = lax.broadcasted_iota(jnp.int32, (COLS, 2 * COLS), 1)

    def lon(w, n):
        high = w.astype(BF16).astype(F32)
        return jnp.where(n < COLS, high, w - high).astype(BF16)

    out = jnp.where(n < COLS, n, n - COLS)
    own = lon(taper(k - out), n)
    k, n, out = k[:32], n[:32], out[:32]
    left, right = lon(taper(k - 32 - out), n), lon(taper(k + COLS - out), n)
    for s in range(4):
        lon_k[s, pl.ds(0, COLS), :] = own
        lon_k[s, pl.ds(COLS, 2 * COLS), :] = jnp.zeros((2 * COLS, 2 * COLS), BF16)
        lon_k[s, pl.ds(COLS + 32 * s, 32), :] = left
        lon_k[s, pl.ds(2 * COLS + 32 * s, 32), :] = right


def kernel(
    h_in, u_in, v_in, observed_in,
    h_out, u_out, v_out, inc,
    x, f, ps, pr, c, rc, lt, ls, lr, g1, lat_k, lon_k, coef, state, s_acc, sq, red,
    observed, strip, relay, relay_x, relay_p,
    load_sem, store_sem, halo_ss, halo_rs, halo_relay_rs, row_ss, row_rs, relay_rs, col_ss, col_rs, red_ss, red_rs,
):
    m = lax.axis_index("member")
    b = lax.axis_index("band")
    has_up = m > 0
    has_dn = m < NMEM - 1
    up = lax.rem(m + NMEM - 1, NMEM)
    dn = lax.rem(m + 1, NMEM)
    lf = lax.rem(b + NBAND - 1, NBAND)
    rt = lax.rem(b + 1, NBAND)

    core = lax.rem(m, 2)
    y = lax.rem(m // 2, 4)
    z_lo = m // 8
    xx = b // 2
    z = lax.rem(b, 2) * 2 + z_lo

    def at(core_, y_, x_, z_):
        return ((lax.rem(z_, 2) * 4 + y_) * 2 + core_, x_ * 2 + z_ // 2)

    stages = [
        [at(1 - core, y, xx, z)],
        [at(core, lax.rem(y + j, 4), xx, z) for j in (1, 2, 3)],
        [at(core, y, lax.rem(xx + j, 4), z) for j in (1, 2, 3)],
        [at(core, y, xx, lax.rem(z + j, 4)) for j in (1, 2, 3)],
    ]

    near = [(up, b), (dn, b), (m, lf), (m, rt), (up, lf), (up, rt), (dn, lf), (dn, rt)]
    mirror = (z_lo * 8 + 7 - lax.rem(m, 8), b)
    greet = near + [mirror] + [d for stage in stages for d in stage]
    barrier = pltpu.get_barrier_semaphore()
    for d in greet:
        pl.semaphore_signal(barrier, inc=1, device_id=d, device_id_type=MESH)

    loads = [
        pltpu.make_async_copy(src, dst, load_sem.at[k])
        for k, (src, dst) in enumerate((
            (h_in, x.at[0, pl.ds(0, MEMBERS), OWN]),
            (u_in, x.at[1, pl.ds(0, MEMBERS), OWN]),
            (v_in, x.at[2, pl.ds(0, MEMBERS), OWN]),
            (observed_in, observed),
        ))
    ]
    for copy in loads:
        copy.start()

    lane = lax.broadcasted_iota(jnp.int32, (ROWS, COLS), 1)

    def pack(g, count):
        left = jnp.zeros((ROWS, COLS), F32)
        right = jnp.zeros((ROWS, COLS), F32)
        for s in range(count):
            base = 16 * s
            i = g * 8 + s
            for field, lo, width in ((1, 0, 6), (0, 6, 5), (2, 11, 5)):
                value = x[field, i, OWN]
                where = (lane >= base + lo) & (lane < base + lo + width)
                left = jnp.where(where, pltpu.roll(value, base + lo, 1), left)
                right = jnp.where(where, pltpu.roll(value, (base + lo + width) % COLS, 1), right)
        ps[0, g, OWN] = left
        ps[1, g, OWN] = right

    def halo_copy(k, n, mean=False):
        members = pl.ds(MEAN, 1) if mean else pl.ds(n * 16, 16)
        groups = pl.ds(MEAN // 8, 1) if mean else pl.ds(n * 2, 2)
        src, dst, to = (
            (x.at[:, members, TOP], x.at[:, members, BELOW], (up, b)),
            (ps.at[:, groups, TOP], ps.at[:, groups, BELOW], (up, b)),
            (ps.at[0, groups, TOP], pr.at[1, groups, BELOW], (up, lf)),
            (ps.at[1, groups, TOP], pr.at[0, groups, BELOW], (up, rt)),
            (x.at[:, members, BOTTOM], x.at[:, members, ABOVE], (dn, b)),
            (ps.at[:, groups, BOTTOM], ps.at[:, groups, ABOVE], (dn, b)),
            (ps.at[0, groups, BOTTOM], pr.at[1, groups, ABOVE], (dn, lf)),
            (ps.at[1, groups, BOTTOM], pr.at[0, groups, ABOVE], (dn, rt)),
            (ps.at[0, groups, OWN], pr.at[1, groups, OWN], (m, lf)),
            (ps.at[1, groups, OWN], pr.at[0, groups, OWN], (m, rt)),
        )[k]
        return pltpu.make_async_remote_copy(
            src_ref=src, dst_ref=dst, send_sem=halo_ss.at[n, k], recv_sem=halo_rs.at[n, k],
            device_id=to, device_id_type=MESH,
        )

    def halo_relay_in(k, n):
        part = k % 4
        return pltpu.make_async_remote_copy(
            src_ref=(x.at[:, pl.ds(n * 16, 16), TOP if k < 4 else BOTTOM] if part == 0
                     else ps.at[:, pl.ds(n * 2, 2), TOP if k < 4 else BOTTOM]),
            dst_ref=(relay_x if part == 0 else relay_p).at[n // 2],
            send_sem=halo_ss.at[n, k], recv_sem=halo_relay_rs.at[n // 2, part],
            device_id=(0 if k < 4 else NMEM - 1, b), device_id_type=MESH,
        )

    def halo_relay_out(k, n):
        part = k % 4
        rows = BELOW if k < 4 else ABOVE
        return pltpu.make_async_remote_copy(
            src_ref=(relay_x if part == 0 else relay_p).at[n // 2],
            dst_ref=x.at[:, pl.ds(n * 16, 16), rows] if part == 0 else ps.at[:, pl.ds(n * 2, 2), rows],
            send_sem=halo_ss.at[n, k], recv_sem=halo_rs.at[n, k],
            device_id=(7 if k < 4 else 8, b), device_id_type=MESH,
        )

    def halo_forward(n):
        for end, ks in ((0, (0, 1)), (NMEM - 1, (4, 5))):

            @pl.when((m == end) & (lax.rem(n, 2) == 1))
            def _(ks=ks):
                for k in ks:
                    halo_relay_in(k, n).wait_recv()
                    halo_relay_out(k, n).start()

    def halo_start(n, mean=False):
        for k in (8, 9):
            halo_copy(k, n, mean).start()
        odd = False if mean else lax.rem(n, 2) == 1
        for there, source, ks in ((has_up, 8, range(0, 4)), (has_dn, 7, range(4, 8))):
            away = (m == source) & odd

            @pl.when(there & jnp.logical_not(away))
            def _(ks=ks):
                for k in ks[:2]:
                    halo_copy(k, n, mean).start()

            if not mean:

                @pl.when(away)
                def _(ks=ks):
                    for k in ks[:2]:
                        halo_relay_in(k, n).start()

            @pl.when(there)
            def _(ks=ks):
                for k in ks[2:]:
                    halo_copy(k, n, mean).start()

    def halo_wait(n, mean=False):
        @pl.when(has_up)
        def _():
            for k in range(4, 8):
                halo_copy(k, n, mean).wait_recv()
            for k in range(0, 4):
                halo_copy(k, n, mean).wait_send()

        @pl.when(has_dn)
        def _():
            for k in range(0, 4):
                halo_copy(k, n, mean).wait_recv()
            for k in range(4, 8):
                halo_copy(k, n, mean).wait_send()

        for k in (8, 9):
            halo_copy(k, n, mean).wait_recv()
            halo_copy(k, n, mean).wait_send()

        if not mean:
            for end, ks in ((0, (0, 1)), (NMEM - 1, (4, 5))):

                @pl.when((m == end) & (lax.rem(n, 2) == 1))
                def _(ks=ks):
                    for k in ks:
                        halo_relay_out(k, n).wait_send()

    def send_halo(n, carry):
        for gg in range(2):
            pack(2 * n + gg, 8)
        halo_start(n)
        return carry

    for copy in loads:
        copy.wait()
    for gg in range(2):
        pack(gg, 8)
    pl.semaphore_wait(barrier, len(greet))
    halo_start(0)

    for k in range(3):
        x[k, MEAN, OWN] = lax.fori_loop(
            0, MEMBERS, lambda i, total, k=k: total + x[k, i, OWN], jnp.zeros((ROWS, COLS), F32), unroll=8
        ) * (1.0 / MEMBERS)
    pack(MEAN // 8, 1)
    halo_start(NHALO, True)

    lax.fori_loop(1, NHALO, send_halo, 0)

    def clear(halo, side):
        x[:, :, halo, :] = jnp.zeros((3, MEMBERS + 8, 6, COLS), F32)
        ps[:, :, halo, :] = jnp.zeros((2, GROUPS, 6, COLS), F32)
        pr[:, :, halo, :] = jnp.zeros((2, GROUPS, 6, COLS), F32)
        for it in range(2):
            rc[it, side] = jnp.zeros((MEMBERS, ROWS, COLS), F32)

    @pl.when(m == 0)
    def _():
        clear(ABOVE, 0)

    @pl.when(m == NMEM - 1)
    def _():
        clear(BELOW, 1)

    build_tapers(lat_k, lon_k)

    tile = lax.broadcasted_iota(jnp.int32, (8, COLS), 0)
    column = lax.broadcasted_iota(jnp.int32, (8, COLS), 1)
    inside = [
        ((6 * tile + j >= 8) | has_up) & ((6 * tile + j < 40) | has_dn) for j in range(6)
    ]
    place = lax.rem(column, 16)
    edge = (column < 6) | (column >= COLS - 6)

    def lon_diff(q):
        return [pltpu.roll(w, COLS - 1, 1) - pltpu.roll(w, 1, 1) for w in q]

    def lat_diff(q):
        out = []
        for first in range(0, len(q), 6):
            part = q[first:first + 6]
            after = part[1:] + [pltpu.roll(part[0], 7, 0)]
            before = [pltpu.roll(part[5], 1, 0)] + part[:5]
            out += [p - w for p, w in zip(after, before)]
        return out

    def advance(hh, uu, vv, keep):
        six = range(len(hh))
        for _ in range(STEPS):
            du, dv = lon_diff(uu), lat_diff(vv)
            hn = [jnp.where(keep[j % 6], hh[j] - 0.2 * (du[j] + dv[j]), 0.0) for j in six]
            dx, dy = lon_diff(hn), lat_diff(hn)
            un = [uu[j] + 0.1 * vv[j] - 0.2 * dx[j] for j in six]
            vn = [jnp.where(inside[j % 6], vv[j] - 0.1 * uu[j] - 0.2 * dy[j], 0.0) for j in six]
            hh, uu, vv = hn, un, vn
        return hh, uu, vv

    def strided(j):
        return pl.ds(j, 8, stride=6)

    def strips(g):
        keep = [w & (place < 12) for w in inside]

        def side(sign, u_shift, h_shift, v_shift, start, u_start):
            far = [pr[sign, g, strided(j)] - ps[1 - sign, g, strided(j)] for j in range(6)]

            def cut(shift, first, width):
                where = (place >= first) & (place < first + width)
                return [jnp.where(where, pltpu.roll(w, shift % COLS, 1) if shift else w, 0.0) for w in far]

            return cut(h_shift, start, 5), cut(u_shift, u_start, 6), cut(v_shift, start, 5)

        left = side(0, 0, -5, -10, 1, 0)
        right = side(1, 6, 0, -5, 6, 6)
        out = advance(*[p + w for p, w in zip(left, right)], keep)
        for k in range(3):
            for j in range(6):
                strip[k, j] = jnp.where(place < 6, out[k][6 + j], out[k][j])

    def forecast(first, s, count):
        out = advance(
            *[[x[k, first + t, strided(j)] for t in range(count) for j in range(6)] for k in range(3)], inside
        )
        for t in range(count):
            shift = (2 * COLS - 6 - 16 * (s + t)) % COLS
            for k in range(3):
                for j in range(6):
                    more = jnp.where(edge, pltpu.roll(strip[k, j], shift, 1), 0.0)
                    f[k, first + t, strided(j)] = out[k][6 * t + j] + more

    halo_wait(NHALO, True)
    strips(MEAN // 8)
    forecast(MEAN, 0, 1)
    mean = [f[k, MEAN, OWN] for k in range(3)]
    for k in range(3):
        state[k] = mean[k]

    def set_coefficients(sh, su, sv):
        residual = observed[pl.ds(ROWS, ROWS)] * (observed[pl.ds(0, ROWS)] - sh - 0.15 * (su * su + sv * sv))
        coef[0] = residual
        coef[1] = 0.3 * su * residual
        coef[2] = 0.3 * sv * residual

    set_coefficients(*mean)

    def row_copy(it, k, n):
        members = pl.ds(n * CHUNK, CHUNK)
        return pltpu.make_async_remote_copy(
            src_ref=c.at[members], dst_ref=rc.at[it, 1 - k, members],
            send_sem=row_ss.at[it, k, n], recv_sem=row_rs.at[it, k, n],
            device_id=near[k], device_id_type=MESH,
        )

    def by_relay(k, n):
        return (m == (8 if k == 0 else 7)) & (lax.rem(n, 2) == 1)

    def at_relay(k, n):
        return (m == (0 if k == 0 else NMEM - 1)) & (lax.rem(n, 2) == 1)

    def relay_in(it, k, n):
        return pltpu.make_async_remote_copy(
            src_ref=c.at[pl.ds(n * CHUNK, CHUNK)], dst_ref=relay.at[it, n // 2],
            send_sem=row_ss.at[it, k, n], recv_sem=relay_rs.at[it, n // 2],
            device_id=(0 if k == 0 else NMEM - 1, b), device_id_type=MESH,
        )

    def relay_out(it, k, n):
        return pltpu.make_async_remote_copy(
            src_ref=relay.at[it, n // 2], dst_ref=rc.at[it, 1 - k, pl.ds(n * CHUNK, CHUNK)],
            send_sem=row_ss.at[it, k, n], recv_sem=row_rs.at[it, k, n],
            device_id=(7 if k == 0 else 8, b), device_id_type=MESH,
        )

    def row_start(it, n):
        for k, there in ((0, has_up), (1, has_dn)):
            pl.when(there & jnp.logical_not(by_relay(k, n)))(row_copy(it, k, n).start)
            pl.when(by_relay(k, n))(relay_in(it, k, n).start)

    def relay_forward(it, n):
        for k in range(2):

            @pl.when(at_relay(k, n))
            def _(k=k):
                relay_in(it, k, n).wait_recv()
                relay_out(it, k, n).start()

    def row_wait(it, n):
        @pl.when(has_up)
        def _():
            row_copy(it, 1, n).wait_recv()

        @pl.when(has_dn)
        def _():
            row_copy(it, 0, n).wait_recv()

    def row_sent(it, n):
        for k, there in ((0, has_up), (1, has_dn)):
            pl.when(there | at_relay(k, n))(row_copy(it, k, n).wait_send)

    def col_copy(it, k, n):
        quads = pl.ds(n * QUADS, QUADS)
        return pltpu.make_async_remote_copy(
            src_ref=ls.at[k, quads], dst_ref=lr.at[it, 1 - k, quads],
            send_sem=col_ss.at[it, k, n], recv_sem=col_rs.at[it, k, n],
            device_id=near[2 + k], device_id_type=MESH,
        )

    scale = 1.0 / math.sqrt(MEMBERS - 1.0)

    def taper_rows(it, n):
        relay_forward(it, n)
        row_wait(it, n)

        for qq in range(QUADS):
            q = n * QUADS + qq
            parts_high, parts_low = [], []
            for ref_part in range(3):
                wide = []
                for s in range(4):
                    i = q * 4 + s
                    wide.append(rc[it, 0, i] if ref_part == 0 else (c[i] if ref_part == 1 else rc[it, 1, i]))
                high, low = split(jnp.concatenate(wide, axis=1))
                parts_high.append(high)
                parts_low.append(low)
            right_side = jnp.concatenate(parts_high + parts_low, axis=0)
            both = jnp.dot(lat_k[...], right_side, preferred_element_type=F32)
            lat = both[:32] + both[32:]
            to_left = jnp.zeros((ROWS, COLS), F32)
            to_right = jnp.zeros((ROWS, COLS), F32)
            for s in range(4):
                part = lat[:, s * COLS:(s + 1) * COLS]
                lt[s, q] = part
                where = (lane >= 32 * s) & (lane < 32 * s + 32)
                to_left = jnp.where(where, pltpu.roll(part, 32 * s, 1) if s else part, to_left)
                to_right = jnp.where(where, pltpu.roll(part, 32 * s + 32, 1) if s < 3 else part, to_right)
            ls[0, q] = to_left
            ls[1, q] = to_right

        for k in range(2):
            col_copy(it, k, n).start()

    def first_chunk(n, carry):
        halo_wait(n)
        pl.when(n + 1 < NHALO)(lambda: halo_forward(n + 1))
        for gg in range(2):
            g = n * 2 + gg
            strips(g)

            for s in range(0, 8, TOGETHER):
                first = g * 8 + s
                forecast(first, s, TOGETHER)
                for t in range(TOGETHER):
                    i = first + t
                    total = None
                    for k in range(3):
                        anomaly = (f[k, i, OWN] - state[k]) * scale
                        x[k, i, OWN] = anomaly
                        term = anomaly * coef[k]
                        total = term if total is None else total + term
                    c[i] = total
            row_start(0, g)

        @pl.when(n >= LAG)
        def _():
            for gg in range(2):
                taper_rows(0, 2 * (n - LAG) + gg)

        return carry

    lax.fori_loop(0, NHALO, first_chunk, 0)

    stores = [
        pltpu.make_async_copy(f.at[k, pl.ds(0, MEMBERS), OWN], dst, store_sem.at[k])
        for k, dst in enumerate((h_out, u_out, v_out))
    ]
    for copy in stores:
        copy.start()

    def taper_cols(it, n, factor):
        for k in range(2):
            col_copy(it, k, n).wait_recv()
        quads = pl.ds(n * QUADS, QUADS)
        size = QUADS * ROWS
        lh, ll = split(lr[it, 0, quads].reshape(size, COLS))
        rhh, rl = split(lr[it, 1, quads].reshape(size, COLS))
        totals = [None] * 4
        for s in range(4):
            mh, ml = split(lt[s, quads].reshape(size, COLS))
            a = jnp.dot(jnp.concatenate([mh, lh, rhh], axis=1), lon_k[s], preferred_element_type=F32)
            d = jnp.dot(jnp.concatenate([ml, ll, rl], axis=1), lon_k[s, :, pl.ds(0, 128)], preferred_element_type=F32)
            g = (a[:, :COLS] + a[:, COLS:] + d).reshape(QUADS, ROWS, COLS)
            if it == 0:
                g1[s, quads] = g
            else:
                g = factor * g1[s, quads] - g
            for qq in range(QUADS):
                i = (n * QUADS + qq) * 4 + s
                part = g[qq]
                terms = [x[k, i, OWN] * part for k in range(3)] + [part * part]
                totals = [t if o is None else o + t for o, t in zip(totals, terms)]
        for k in range(3):
            s_acc[it, k] += totals[k]
        sq[...] += totals[3]

    def localize(it, factor):
        early, behind = (NCHUNK - 2 * LAG, BEHIND) if it == 0 else (0, SKEW)

        def body(n, carry):
            @pl.when(n + early < NCHUNK)
            def _():
                taper_rows(it, n + early)

            @pl.when(n >= behind)
            def _():
                taper_cols(it, n - behind, factor)

            return carry

        lax.fori_loop(0, NCHUNK + behind, body, 0)

    def sum_all(it):
        value = sq[...]
        value = value[:8] + value[8:16] + value[16:24] + value[24:]
        slot = 0
        started = []
        for stage in stages:
            red[it, slot] = value
            copies = [
                pltpu.make_async_remote_copy(
                    src_ref=red.at[it, slot], dst_ref=red.at[it, slot + 1 + j],
                    send_sem=red_ss.at[it, slot + j], recv_sem=red_rs.at[it, slot + j],
                    device_id=d, device_id_type=MESH,
                )
                for j, d in enumerate(stage)
            ]
            for copy in copies:
                copy.start()
            for copy in copies:
                copy.wait_recv()
            for j in range(len(stage)):
                value = value + red[it, slot + 1 + j]
            started.extend(copies)
            slot += 1 + len(stage)
        for copy in started:
            copy.wait_send()
        total = jnp.sum(jnp.sum(value, axis=0, keepdims=True), axis=1, keepdims=True)
        return observed[pl.ds(2 * ROWS + 8 * it, 1), pl.ds(0, 1)] / jnp.sqrt(total / CELLS + 1e-6)

    for it in range(2):
        for k in range(3):
            s_acc[it, k] = jnp.zeros((ROWS, COLS), F32)
    sq[...] = jnp.zeros((ROWS, COLS), F32)
    localize(0, None)
    factor1 = sum_all(0)

    def sent(n, carry):
        row_sent(0, n)
        for k in range(2):
            col_copy(0, k, n).wait_send()
        return carry

    lax.fori_loop(0, NCHUNK, sent, 0)
    sq[...] = jnp.zeros((ROWS, COLS), F32)
    set_coefficients(*[state[k] + factor1 * s_acc[0, k] for k in range(3)])

    def second_chunk(n, carry):
        def one(j, carry2):
            i = n * CHUNK + j
            c[i] = x[0, i, OWN] * coef[0] + x[1, i, OWN] * coef[1] + x[2, i, OWN] * coef[2]
            return carry2

        lax.fori_loop(0, CHUNK, one, 0, unroll=4)
        row_start(1, n)
        return carry

    lax.fori_loop(0, NCHUNK, second_chunk, 0)
    localize(1, factor1)
    factor2 = sum_all(1)
    for k in range(3):
        inc[k] = factor1 * s_acc[0, k] - factor2 * s_acc[1, k]

    def sent2(n, carry):
        row_sent(1, n)
        for k in range(2):
            col_copy(1, k, n).wait_send()
        return carry

    lax.fori_loop(0, NCHUNK, sent2, 0)
    for copy in stores:
        copy.wait()


def per_device(height, east, north, obs_value, obs_mask, obs_precision, step_sizes):
    block = (MEMBERS, ROWS, COLS)
    vmem = pl.BlockSpec(memory_space=pltpu.VMEM)
    anyspace = pl.BlockSpec(memory_space=pl.ANY)
    dma = pltpu.SemaphoreType.DMA
    steps = jnp.broadcast_to((step_sizes.astype(F32) / 64.0)[:, None, None], (2, 8, COLS))
    observed = jnp.concatenate(
        [obs_value, obs_mask.astype(F32) * obs_precision, steps.reshape(16, COLS)], axis=0
    )
    h, u, v, inc = pl.pallas_call(
        kernel,
        name="analysis",
        out_shape=[jax.ShapeDtypeStruct(block, F32)] * 3 + [jax.ShapeDtypeStruct((3, ROWS, COLS), F32)],
        in_specs=[pl.BlockSpec(memory_space=pltpu.HBM)] * 4,
        out_specs=[anyspace] * 3 + [vmem],
        scratch_shapes=[
            pltpu.VMEM((3, MEMBERS + 8, 48, COLS), F32),
            pltpu.VMEM((3, MEMBERS + 1, 48, COLS), F32),
            pltpu.VMEM((2, GROUPS, 48, COLS), F32),
            pltpu.VMEM((2, GROUPS, 48, COLS), F32),
            pltpu.VMEM(block, F32),
            pltpu.VMEM((2, 2) + block, F32),
            pltpu.VMEM((4, MEMBERS // 4, ROWS, COLS), F32),
            pltpu.VMEM((2, MEMBERS // 4, ROWS, COLS), F32),
            pltpu.VMEM((2, 2, MEMBERS // 4, ROWS, COLS), F32),
            pltpu.VMEM((4, MEMBERS // 4, ROWS, COLS), F32),
            pltpu.VMEM((64, 192), BF16),
            pltpu.VMEM((4, 384, 256), BF16),
            pltpu.VMEM((3, ROWS, COLS), F32),
            pltpu.VMEM((3, ROWS, COLS), F32),
            pltpu.VMEM((2, 3, ROWS, COLS), F32),
            pltpu.VMEM((ROWS, COLS), F32),
            pltpu.VMEM((2, 14, 8, COLS), F32),
            pltpu.VMEM((2 * ROWS + 16, COLS), F32),
            pltpu.VMEM((3, 6, 8, COLS), F32),
            pltpu.VMEM((2, NCHUNK // 2, CHUNK, ROWS, COLS), F32),
            pltpu.VMEM((NHALO // 2, 3, 16, 6, COLS), F32),
            pltpu.VMEM((NHALO // 2, 2, 2, 6, COLS), F32),
            dma((4,)), dma((3,)),
            dma((NHALO + 1, 10)), dma((NHALO + 1, 10)), dma((NHALO // 2, 2)),
            dma((2, 2, NCHUNK)), dma((2, 2, NCHUNK)), dma((2, NCHUNK // 2)),
            dma((2, 2, NCHUNK)), dma((2, 2, NCHUNK)),
            dma((2, 14)), dma((2, 14)),
        ],
        compiler_params=pltpu.CompilerParams(
            collective_id=0, has_side_effects=True, vmem_limit_bytes=50 << 20
        ),
    )(height, east, north, observed)
    return h + inc[0], u + inc[1], v + inc[2]


def solution(mesh):
    spec3 = P(None, "member", "band")
    spec2 = P("member", "band")
    return jax.shard_map(
        per_device,
        mesh=mesh,
        in_specs=(spec3, spec3, spec3, spec2, spec2, spec2, P()),
        out_specs=(spec3, spec3, spec3),
        check_vma=False,
    )
```

```python
import functools
import math

import jax
import jax.numpy as jnp
from jax import lax
from jax.experimental import pallas as pl
from jax.experimental.pallas import tpu as pltpu
from jax.sharding import PartitionSpec as P

MESH = pl.DeviceIdType.MESH
F32 = jnp.float32
BF16 = jnp.bfloat16

MEMBERS = 80
ROWS = 32
COLS = 128
NMEM = 16
NBAND = 8
STEPS = 3
LSCALE = 12.0
REACH = 32
GROUPS = 11
MEAN = 80
CHUNK = 8
NCHUNK = MEMBERS // CHUNK
QUADS = CHUNK // 4
NHALO = MEMBERS // 16
SKEW = 4
LAG = 3
BEHIND = 5
TOGETHER = 8
ABOVE, OWN, BELOW = pl.ds(2, 6), pl.ds(8, 32), pl.ds(40, 6)
TOP, BOTTOM = pl.ds(8, 6), pl.ds(34, 6)
CELLS = float(MEMBERS * 512 * 1024)


def taper(offset):
    scaled = offset.astype(F32) / LSCALE
    weight = jnp.exp(-0.5 * scaled * scaled)
    return jnp.where(jnp.abs(offset) <= REACH, weight, 0.0)


def split(x):
    high = x.astype(BF16)
    low = (x - high.astype(F32)).astype(BF16)
    return high, low


def build_tapers(lat_k, lon_k):
    i = lax.broadcasted_iota(jnp.int32, (64, 192), 0)
    j = lax.broadcasted_iota(jnp.int32, (64, 192), 1)
    a = jnp.where(i < 32, i, i - 32)
    jj = jnp.where(j < 96, j, j - 96)
    w = taper(jj - 32 - a)
    high = w.astype(BF16).astype(F32)
    low = jnp.where(j < 96, w - high, 0.0)
    lat_k[...] = jnp.where(i < 32, high, low).astype(BF16)
    k = lax.broadcasted_iota(jnp.int32, (COLS, 2 * COLS), 0)
    n = lax.broadcasted_iota(jnp.int32, (COLS, 2 * COLS), 1)

    def lon(w, n):
        high = w.astype(BF16).astype(F32)
        return jnp.where(n < COLS, high, w - high).astype(BF16)

    out = jnp.where(n < COLS, n, n - COLS)
    own = lon(taper(k - out), n)
    k, n, out = k[:32], n[:32], out[:32]
    left, right = lon(taper(k - 32 - out), n), lon(taper(k + COLS - out), n)
    for s in range(4):
        lon_k[s, pl.ds(0, COLS), :] = own
        lon_k[s, pl.ds(COLS, 2 * COLS), :] = jnp.zeros((2 * COLS, 2 * COLS), BF16)
        lon_k[s, pl.ds(COLS + 32 * s, 32), :] = left
        lon_k[s, pl.ds(2 * COLS + 32 * s, 32), :] = right


def kernel(
    h_in, u_in, v_in, observed_in,
    h_out, u_out, v_out, inc,
    x, f, ps, pr, c, rc, lt, ls, lr, g1, lat_k, lon_k, coef, state, s_acc, sq, red,
    observed, strip, relay, relay_x, relay_p,
    load_sem, store_sem, halo_ss, halo_rs, halo_relay_rs, row_ss, row_rs, relay_rs, col_ss, col_rs, red_ss, red_rs,
):
    m = lax.axis_index("member")
    b = lax.axis_index("band")
    has_up = m > 0
    has_dn = m < NMEM - 1
    up = lax.rem(m + NMEM - 1, NMEM)
    dn = lax.rem(m + 1, NMEM)
    lf = lax.rem(b + NBAND - 1, NBAND)
    rt = lax.rem(b + 1, NBAND)

    core = lax.rem(m, 2)
    y = lax.rem(m // 2, 4)
    z_lo = m // 8
    xx = b // 2
    z = lax.rem(b, 2) * 2 + z_lo

    def at(core_, y_, x_, z_):
        return ((lax.rem(z_, 2) * 4 + y_) * 2 + core_, x_ * 2 + z_ // 2)

    stages = [
        [at(1 - core, y, xx, z)],
        [at(core, lax.rem(y + j, 4), xx, z) for j in (1, 2, 3)],
        [at(core, y, lax.rem(xx + j, 4), z) for j in (1, 2, 3)],
        [at(core, y, xx, lax.rem(z + j, 4)) for j in (1, 2, 3)],
    ]

    near = [(up, b), (dn, b), (m, lf), (m, rt), (up, lf), (up, rt), (dn, lf), (dn, rt)]
    mirror = (z_lo * 8 + 7 - lax.rem(m, 8), b)
    greet = near + [mirror] + [d for stage in stages for d in stage]
    barrier = pltpu.get_barrier_semaphore()
    for d in greet:
        pl.semaphore_signal(barrier, inc=1, device_id=d, device_id_type=MESH)

    loads = [
        pltpu.make_async_copy(src, dst, load_sem.at[k])
        for k, (src, dst) in enumerate((
            (h_in, x.at[0, pl.ds(0, MEMBERS), OWN]),
            (u_in, x.at[1, pl.ds(0, MEMBERS), OWN]),
            (v_in, x.at[2, pl.ds(0, MEMBERS), OWN]),
            (observed_in, observed),
        ))
    ]
    for copy in loads:
        copy.start()

    lane = lax.broadcasted_iota(jnp.int32, (ROWS, COLS), 1)

    def pack(g, count):
        left = jnp.zeros((ROWS, COLS), F32)
        right = jnp.zeros((ROWS, COLS), F32)
        for s in range(count):
            base = 16 * s
            i = g * 8 + s
            for field, lo, width in ((1, 0, 6), (0, 6, 5), (2, 11, 5)):
                value = x[field, i, OWN]
                where = (lane >= base + lo) & (lane < base + lo + width)
                left = jnp.where(where, pltpu.roll(value, base + lo, 1), left)
                right = jnp.where(where, pltpu.roll(value, (base + lo + width) % COLS, 1), right)
        ps[0, g, OWN] = left
        ps[1, g, OWN] = right

    def halo_copy(k, n, mean=False):
        members = pl.ds(MEAN, 1) if mean else pl.ds(n * 16, 16)
        groups = pl.ds(MEAN // 8, 1) if mean else pl.ds(n * 2, 2)
        src, dst, to = (
            (x.at[:, members, TOP], x.at[:, members, BELOW], (up, b)),
            (ps.at[:, groups, TOP], ps.at[:, groups, BELOW], (up, b)),
            (ps.at[0, groups, TOP], pr.at[1, groups, BELOW], (up, lf)),
            (ps.at[1, groups, TOP], pr.at[0, groups, BELOW], (up, rt)),
            (x.at[:, members, BOTTOM], x.at[:, members, ABOVE], (dn, b)),
            (ps.at[:, groups, BOTTOM], ps.at[:, groups, ABOVE], (dn, b)),
            (ps.at[0, groups, BOTTOM], pr.at[1, groups, ABOVE], (dn, lf)),
            (ps.at[1, groups, BOTTOM], pr.at[0, groups, ABOVE], (dn, rt)),
            (ps.at[0, groups, OWN], pr.at[1, groups, OWN], (m, lf)),
            (ps.at[1, groups, OWN], pr.at[0, groups, OWN], (m, rt)),
        )[k]
        return pltpu.make_async_remote_copy(
            src_ref=src, dst_ref=dst, send_sem=halo_ss.at[n, k], recv_sem=halo_rs.at[n, k],
            device_id=to, device_id_type=MESH,
        )

    def halo_relay_in(k, n):
        part = k % 4
        return pltpu.make_async_remote_copy(
            src_ref=(x.at[:, pl.ds(n * 16, 16), TOP if k < 4 else BOTTOM] if part == 0
                     else ps.at[:, pl.ds(n * 2, 2), TOP if k < 4 else BOTTOM]),
            dst_ref=(relay_x if part == 0 else relay_p).at[n // 2],
            send_sem=halo_ss.at[n, k], recv_sem=halo_relay_rs.at[n // 2, part],
            device_id=(0 if k < 4 else NMEM - 1, b), device_id_type=MESH,
        )

    def halo_relay_out(k, n):
        part = k % 4
        rows = BELOW if k < 4 else ABOVE
        return pltpu.make_async_remote_copy(
            src_ref=(relay_x if part == 0 else relay_p).at[n // 2],
            dst_ref=x.at[:, pl.ds(n * 16, 16), rows] if part == 0 else ps.at[:, pl.ds(n * 2, 2), rows],
            send_sem=halo_ss.at[n, k], recv_sem=halo_rs.at[n, k],
            device_id=(7 if k < 4 else 8, b), device_id_type=MESH,
        )

    def halo_forward(n):
        for end, ks in ((0, (0, 1)), (NMEM - 1, (4, 5))):

            @pl.when((m == end) & (lax.rem(n, 2) == 1))
            def _(ks=ks):
                for k in ks:
                    halo_relay_in(k, n).wait_recv()
                    halo_relay_out(k, n).start()

    def halo_start(n, mean=False):
        for k in (8, 9):
            halo_copy(k, n, mean).start()
        odd = False if mean else lax.rem(n, 2) == 1
        for there, source, ks in ((has_up, 8, range(0, 4)), (has_dn, 7, range(4, 8))):
            away = (m == source) & odd

            @pl.when(there & jnp.logical_not(away))
            def _(ks=ks):
                for k in ks[:2]:
                    halo_copy(k, n, mean).start()

            if not mean:

                @pl.when(away)
                def _(ks=ks):
                    for k in ks[:2]:
                        halo_relay_in(k, n).start()

            @pl.when(there)
            def _(ks=ks):
                for k in ks[2:]:
                    halo_copy(k, n, mean).start()

    def halo_wait(n, mean=False):
        @pl.when(has_up)
        def _():
            for k in range(4, 8):
                halo_copy(k, n, mean).wait_recv()
            for k in range(0, 4):
                halo_copy(k, n, mean).wait_send()

        @pl.when(has_dn)
        def _():
            for k in range(0, 4):
                halo_copy(k, n, mean).wait_recv()
            for k in range(4, 8):
                halo_copy(k, n, mean).wait_send()

        for k in (8, 9):
            halo_copy(k, n, mean).wait_recv()
            halo_copy(k, n, mean).wait_send()

        if not mean:
            for end, ks in ((0, (0, 1)), (NMEM - 1, (4, 5))):

                @pl.when((m == end) & (lax.rem(n, 2) == 1))
                def _(ks=ks):
                    for k in ks:
                        halo_relay_out(k, n).wait_send()

    def send_halo(n, carry):
        for gg in range(2):
            pack(2 * n + gg, 8)
        halo_start(n)
        return carry

    for copy in loads:
        copy.wait()
    for gg in range(2):
        pack(gg, 8)
    pl.semaphore_wait(barrier, len(greet))
    halo_start(0)

    for k in range(3):
        x[k, MEAN, OWN] = lax.fori_loop(
            0, MEMBERS, lambda i, total, k=k: total + x[k, i, OWN], jnp.zeros((ROWS, COLS), F32), unroll=8
        ) * (1.0 / MEMBERS)
    pack(MEAN // 8, 1)
    halo_start(NHALO, True)

    lax.fori_loop(1, NHALO, send_halo, 0)

    def clear(halo, side):
        x[:, :, halo, :] = jnp.zeros((3, MEMBERS + 8, 6, COLS), F32)
        ps[:, :, halo, :] = jnp.zeros((2, GROUPS, 6, COLS), F32)
        pr[:, :, halo, :] = jnp.zeros((2, GROUPS, 6, COLS), F32)
        for it in range(2):
            rc[it, side] = jnp.zeros((MEMBERS, ROWS, COLS), F32)

    @pl.when(m == 0)
    def _():
        clear(ABOVE, 0)

    @pl.when(m == NMEM - 1)
    def _():
        clear(BELOW, 1)

    build_tapers(lat_k, lon_k)

    tile = lax.broadcasted_iota(jnp.int32, (8, COLS), 0)
    column = lax.broadcasted_iota(jnp.int32, (8, COLS), 1)
    inside = [
        ((6 * tile + j >= 8) | has_up) & ((6 * tile + j < 40) | has_dn) for j in range(6)
    ]
    place = lax.rem(column, 16)
    edge = (column < 6) | (column >= COLS - 6)

    def lon_diff(q):
        return [pltpu.roll(w, COLS - 1, 1) - pltpu.roll(w, 1, 1) for w in q]

    def lat_diff(q):
        out = []
        for first in range(0, len(q), 6):
            part = q[first:first + 6]
            after = part[1:] + [pltpu.roll(part[0], 7, 0)]
            before = [pltpu.roll(part[5], 1, 0)] + part[:5]
            out += [p - w for p, w in zip(after, before)]
        return out

    def advance(hh, uu, vv, keep):
        six = range(len(hh))
        for _ in range(STEPS):
            du, dv = lon_diff(uu), lat_diff(vv)
            hn = [jnp.where(keep[j % 6], hh[j] - 0.2 * (du[j] + dv[j]), 0.0) for j in six]
            dx, dy = lon_diff(hn), lat_diff(hn)
            un = [uu[j] + 0.1 * vv[j] - 0.2 * dx[j] for j in six]
            vn = [jnp.where(inside[j % 6], vv[j] - 0.1 * uu[j] - 0.2 * dy[j], 0.0) for j in six]
            hh, uu, vv = hn, un, vn
        return hh, uu, vv

    def strided(j):
        return pl.ds(j, 8, stride=6)

    def strips(g):
        keep = [w & (place < 12) for w in inside]

        def side(sign, u_shift, h_shift, v_shift, start, u_start):
            far = [pr[sign, g, strided(j)] - ps[1 - sign, g, strided(j)] for j in range(6)]

            def cut(shift, first, width):
                where = (place >= first) & (place < first + width)
                return [jnp.where(where, pltpu.roll(w, shift % COLS, 1) if shift else w, 0.0) for w in far]

            return cut(h_shift, start, 5), cut(u_shift, u_start, 6), cut(v_shift, start, 5)

        left = side(0, 0, -5, -10, 1, 0)
        right = side(1, 6, 0, -5, 6, 6)
        out = advance(*[p + w for p, w in zip(left, right)], keep)
        for k in range(3):
            for j in range(6):
                strip[k, j] = jnp.where(place < 6, out[k][6 + j], out[k][j])

    def forecast(first, s, count):
        out = advance(
            *[[x[k, first + t, strided(j)] for t in range(count) for j in range(6)] for k in range(3)], inside
        )
        for t in range(count):
            shift = (2 * COLS - 6 - 16 * (s + t)) % COLS
            for k in range(3):
                for j in range(6):
                    more = jnp.where(edge, pltpu.roll(strip[k, j], shift, 1), 0.0)
                    f[k, first + t, strided(j)] = out[k][6 * t + j] + more

    halo_wait(NHALO, True)
    strips(MEAN // 8)
    forecast(MEAN, 0, 1)
    mean = [f[k, MEAN, OWN] for k in range(3)]
    for k in range(3):
        state[k] = mean[k]

    def set_coefficients(sh, su, sv):
        residual = observed[pl.ds(ROWS, ROWS)] * (observed[pl.ds(0, ROWS)] - sh - 0.15 * (su * su + sv * sv))
        coef[0] = residual
        coef[1] = 0.3 * su * residual
        coef[2] = 0.3 * sv * residual

    set_coefficients(*mean)

    def row_copy(it, k, n):
        members = pl.ds(n * CHUNK, CHUNK)
        return pltpu.make_async_remote_copy(
            src_ref=c.at[members], dst_ref=rc.at[it, 1 - k, members],
            send_sem=row_ss.at[it, k, n], recv_sem=row_rs.at[it, k, n],
            device_id=near[k], device_id_type=MESH,
        )

    def by_relay(k, n):
        return (m == (8 if k == 0 else 7)) & (lax.rem(n, 2) == 1)

    def at_relay(k, n):
        return (m == (0 if k == 0 else NMEM - 1)) & (lax.rem(n, 2) == 1)

    def relay_in(it, k, n):
        return pltpu.make_async_remote_copy(
            src_ref=c.at[pl.ds(n * CHUNK, CHUNK)], dst_ref=relay.at[it, n // 2],
            send_sem=row_ss.at[it, k, n], recv_sem=relay_rs.at[it, n // 2],
            device_id=(0 if k == 0 else NMEM - 1, b), device_id_type=MESH,
        )

    def relay_out(it, k, n):
        return pltpu.make_async_remote_copy(
            src_ref=relay.at[it, n // 2], dst_ref=rc.at[it, 1 - k, pl.ds(n * CHUNK, CHUNK)],
            send_sem=row_ss.at[it, k, n], recv_sem=row_rs.at[it, k, n],
            device_id=(7 if k == 0 else 8, b), device_id_type=MESH,
        )

    def row_start(it, n):
        for k, there in ((0, has_up), (1, has_dn)):
            pl.when(there & jnp.logical_not(by_relay(k, n)))(row_copy(it, k, n).start)
            pl.when(by_relay(k, n))(relay_in(it, k, n).start)

    def relay_forward(it, n):
        for k in range(2):

            @pl.when(at_relay(k, n))
            def _(k=k):
                relay_in(it, k, n).wait_recv()
                relay_out(it, k, n).start()

    def row_wait(it, n):
        @pl.when(has_up)
        def _():
            row_copy(it, 1, n).wait_recv()

        @pl.when(has_dn)
        def _():
            row_copy(it, 0, n).wait_recv()

    def row_sent(it, n):
        for k, there in ((0, has_up), (1, has_dn)):
            pl.when(there | at_relay(k, n))(row_copy(it, k, n).wait_send)

    def col_copy(it, k, n):
        quads = pl.ds(n * QUADS, QUADS)
        return pltpu.make_async_remote_copy(
            src_ref=ls.at[k, quads], dst_ref=lr.at[it, 1 - k, quads],
            send_sem=col_ss.at[it, k, n], recv_sem=col_rs.at[it, k, n],
            device_id=near[2 + k], device_id_type=MESH,
        )

    scale = 1.0 / math.sqrt(MEMBERS - 1.0)

    def taper_rows(it, n):
        row_wait(it, n)
        pl.when(n + 1 < NCHUNK)(lambda: relay_forward(it, n + 1))

        for qq in range(QUADS):
            q = n * QUADS + qq
            parts_high, parts_low = [], []
            for ref_part in range(3):
                wide = []
                for s in range(4):
                    i = q * 4 + s
                    wide.append(rc[it, 0, i] if ref_part == 0 else (c[i] if ref_part == 1 else rc[it, 1, i]))
                high, low = split(jnp.concatenate(wide, axis=1))
                parts_high.append(high)
                parts_low.append(low)
            right_side = jnp.concatenate(parts_high + parts_low, axis=0)
            both = jnp.dot(lat_k[...], right_side, preferred_element_type=F32)
            lat = both[:32] + both[32:]
            to_left = jnp.zeros((ROWS, COLS), F32)
            to_right = jnp.zeros((ROWS, COLS), F32)
            for s in range(4):
                part = lat[:, s * COLS:(s + 1) * COLS]
                lt[s, q] = part
                where = (lane >= 32 * s) & (lane < 32 * s + 32)
                to_left = jnp.where(where, pltpu.roll(part, 32 * s, 1) if s else part, to_left)
                to_right = jnp.where(where, pltpu.roll(part, 32 * s + 32, 1) if s < 3 else part, to_right)
            ls[0, q] = to_left
            ls[1, q] = to_right

        for k in range(2):
            col_copy(it, k, n).start()

    def first_chunk(n, carry):
        halo_wait(n)
        pl.when(n + 1 < NHALO)(lambda: halo_forward(n + 1))
        for gg in range(2):
            g = n * 2 + gg
            strips(g)

            for s in range(0, 8, TOGETHER):
                first = g * 8 + s
                forecast(first, s, TOGETHER)
                for t in range(TOGETHER):
                    i = first + t
                    total = None
                    for k in range(3):
                        anomaly = (f[k, i, OWN] - state[k]) * scale
                        x[k, i, OWN] = anomaly
                        term = anomaly * coef[k]
                        total = term if total is None else total + term
                    c[i] = total
            row_start(0, g)

        @pl.when(n >= LAG)
        def _():
            for gg in range(2):
                taper_rows(0, 2 * (n - LAG) + gg)

        return carry

    lax.fori_loop(0, NHALO, first_chunk, 0)

    stores = [
        pltpu.make_async_copy(f.at[k, pl.ds(0, MEMBERS), OWN], dst, store_sem.at[k])
        for k, dst in enumerate((h_out, u_out, v_out))
    ]
    for copy in stores:
        copy.start()

    def taper_cols(it, n, factor):
        for k in range(2):
            col_copy(it, k, n).wait_recv()
        quads = pl.ds(n * QUADS, QUADS)
        size = QUADS * ROWS
        lh, ll = split(lr[it, 0, quads].reshape(size, COLS))
        rhh, rl = split(lr[it, 1, quads].reshape(size, COLS))
        totals = [None] * 4
        for s in range(4):
            mh, ml = split(lt[s, quads].reshape(size, COLS))
            a = jnp.dot(jnp.concatenate([mh, lh, rhh], axis=1), lon_k[s], preferred_element_type=F32)
            d = jnp.dot(jnp.concatenate([ml, ll, rl], axis=1), lon_k[s, :, pl.ds(0, 128)], preferred_element_type=F32)
            g = (a[:, :COLS] + a[:, COLS:] + d).reshape(QUADS, ROWS, COLS)
            if it == 0:
                g1[s, quads] = g
            else:
                g = factor * g1[s, quads] - g
            for qq in range(QUADS):
                i = (n * QUADS + qq) * 4 + s
                part = g[qq]
                terms = [x[k, i, OWN] * part for k in range(3)] + [part * part]
                totals = [t if o is None else o + t for o, t in zip(totals, terms)]
        for k in range(3):
            s_acc[it, k] += totals[k]
        sq[...] += totals[3]

    def localize(it, factor):
        early, behind = (NCHUNK - 2 * LAG, BEHIND) if it == 0 else (0, SKEW)

        def body(n, carry):
            @pl.when(n + early < NCHUNK)
            def _():
                taper_rows(it, n + early)

            @pl.when(n >= behind)
            def _():
                taper_cols(it, n - behind, factor)

            return carry

        lax.fori_loop(0, NCHUNK + behind, body, 0)

    def sum_all(it):
        value = sq[...]
        value = value[:8] + value[8:16] + value[16:24] + value[24:]
        slot = 0
        started = []
        for stage in stages:
            red[it, slot] = value
            copies = [
                pltpu.make_async_remote_copy(
                    src_ref=red.at[it, slot], dst_ref=red.at[it, slot + 1 + j],
                    send_sem=red_ss.at[it, slot + j], recv_sem=red_rs.at[it, slot + j],
                    device_id=d, device_id_type=MESH,
                )
                for j, d in enumerate(stage)
            ]
            for copy in copies:
                copy.start()
            for copy in copies:
                copy.wait_recv()
            for j in range(len(stage)):
                value = value + red[it, slot + 1 + j]
            started.extend(copies)
            slot += 1 + len(stage)
        for copy in started:
            copy.wait_send()
        total = jnp.sum(jnp.sum(value, axis=0, keepdims=True), axis=1, keepdims=True)
        return observed[pl.ds(2 * ROWS + 8 * it, 1), pl.ds(0, 1)] / jnp.sqrt(total / CELLS + 1e-6)

    for it in range(2):
        for k in range(3):
            s_acc[it, k] = jnp.zeros((ROWS, COLS), F32)
    sq[...] = jnp.zeros((ROWS, COLS), F32)
    localize(0, None)
    factor1 = sum_all(0)

    def sent(n, carry):
        row_sent(0, n)
        for k in range(2):
            col_copy(0, k, n).wait_send()
        return carry

    lax.fori_loop(0, NCHUNK, sent, 0)
    sq[...] = jnp.zeros((ROWS, COLS), F32)
    set_coefficients(*[state[k] + factor1 * s_acc[0, k] for k in range(3)])

    def second_chunk(n, carry):
        def one(j, carry2):
            i = n * CHUNK + j
            c[i] = x[0, i, OWN] * coef[0] + x[1, i, OWN] * coef[1] + x[2, i, OWN] * coef[2]
            return carry2

        lax.fori_loop(0, CHUNK, one, 0, unroll=4)
        row_start(1, n)
        return carry

    lax.fori_loop(0, NCHUNK, second_chunk, 0)
    localize(1, factor1)
    factor2 = sum_all(1)
    for k in range(3):
        inc[k] = factor1 * s_acc[0, k] - factor2 * s_acc[1, k]

    def sent2(n, carry):
        row_sent(1, n)
        for k in range(2):
            col_copy(1, k, n).wait_send()
        return carry

    lax.fori_loop(0, NCHUNK, sent2, 0)
    for copy in stores:
        copy.wait()


def per_device(height, east, north, obs_value, obs_mask, obs_precision, step_sizes):
    block = (MEMBERS, ROWS, COLS)
    vmem = pl.BlockSpec(memory_space=pltpu.VMEM)
    anyspace = pl.BlockSpec(memory_space=pl.ANY)
    dma = pltpu.SemaphoreType.DMA
    steps = jnp.broadcast_to((step_sizes.astype(F32) / 64.0)[:, None, None], (2, 8, COLS))
    observed = jnp.concatenate(
        [obs_value, obs_mask.astype(F32) * obs_precision, steps.reshape(16, COLS)], axis=0
    )
    h, u, v, inc = pl.pallas_call(
        kernel,
        name="analysis",
        out_shape=[jax.ShapeDtypeStruct(block, F32)] * 3 + [jax.ShapeDtypeStruct((3, ROWS, COLS), F32)],
        in_specs=[pl.BlockSpec(memory_space=pltpu.HBM)] * 4,
        out_specs=[anyspace] * 3 + [vmem],
        scratch_shapes=[
            pltpu.VMEM((3, MEMBERS + 8, 48, COLS), F32),
            pltpu.VMEM((3, MEMBERS + 1, 48, COLS), F32),
            pltpu.VMEM((2, GROUPS, 48, COLS), F32),
            pltpu.VMEM((2, GROUPS, 48, COLS), F32),
            pltpu.VMEM(block, F32),
            pltpu.VMEM((2, 2) + block, F32),
            pltpu.VMEM((4, MEMBERS // 4, ROWS, COLS), F32),
            pltpu.VMEM((2, MEMBERS // 4, ROWS, COLS), F32),
            pltpu.VMEM((2, 2, MEMBERS // 4, ROWS, COLS), F32),
            pltpu.VMEM((4, MEMBERS // 4, ROWS, COLS), F32),
            pltpu.VMEM((64, 192), BF16),
            pltpu.VMEM((4, 384, 256), BF16),
            pltpu.VMEM((3, ROWS, COLS), F32),
            pltpu.VMEM((3, ROWS, COLS), F32),
            pltpu.VMEM((2, 3, ROWS, COLS), F32),
            pltpu.VMEM((ROWS, COLS), F32),
            pltpu.VMEM((2, 14, 8, COLS), F32),
            pltpu.VMEM((2 * ROWS + 16, COLS), F32),
            pltpu.VMEM((3, 6, 8, COLS), F32),
            pltpu.VMEM((2, NCHUNK // 2, CHUNK, ROWS, COLS), F32),
            pltpu.VMEM((NHALO // 2, 3, 16, 6, COLS), F32),
            pltpu.VMEM((NHALO // 2, 2, 2, 6, COLS), F32),
            dma((4,)), dma((3,)),
            dma((NHALO + 1, 10)), dma((NHALO + 1, 10)), dma((NHALO // 2, 2)),
            dma((2, 2, NCHUNK)), dma((2, 2, NCHUNK)), dma((2, NCHUNK // 2)),
            dma((2, 2, NCHUNK)), dma((2, 2, NCHUNK)),
            dma((2, 14)), dma((2, 14)),
        ],
        compiler_params=pltpu.CompilerParams(
            collective_id=0, has_side_effects=True, vmem_limit_bytes=50 << 20
        ),
    )(height, east, north, observed)
    return h + inc[0], u + inc[1], v + inc[2]


def solution(mesh):
    spec3 = P(None, "member", "band")
    spec2 = P("member", "band")
    return jax.shard_map(
        per_device,
        mesh=mesh,
        in_specs=(spec3, spec3, spec3, spec2, spec2, spec2, P()),
        out_specs=(spec3, spec3, spec3),
        check_vma=False,
    )
```

```python
import functools
import math

import jax
import jax.numpy as jnp
from jax import lax
from jax.experimental import pallas as pl
from jax.experimental.pallas import tpu as pltpu
from jax.sharding import PartitionSpec as P

MESH = pl.DeviceIdType.MESH
F32 = jnp.float32
BF16 = jnp.bfloat16

MEMBERS = 80
ROWS = 32
COLS = 128
NMEM = 16
NBAND = 8
STEPS = 3
LSCALE = 12.0
REACH = 32
GROUPS = 11
MEAN = 80
CHUNK = 8
NCHUNK = MEMBERS // CHUNK
QUADS = CHUNK // 4
NHALO = MEMBERS // 16
SKEW = 4
LAG = 3
BEHIND = 5
TOGETHER = 8
ABOVE, OWN, BELOW = pl.ds(2, 6), pl.ds(8, 32), pl.ds(40, 6)
TOP, BOTTOM = pl.ds(8, 6), pl.ds(34, 6)
CELLS = float(MEMBERS * 512 * 1024)


def taper(offset):
    scaled = offset.astype(F32) / LSCALE
    weight = jnp.exp(-0.5 * scaled * scaled)
    return jnp.where(jnp.abs(offset) <= REACH, weight, 0.0)


def split(x):
    high = x.astype(BF16)
    low = (x - high.astype(F32)).astype(BF16)
    return high, low


def build_tapers(lat_k, lon_k):
    i = lax.broadcasted_iota(jnp.int32, (64, 192), 0)
    j = lax.broadcasted_iota(jnp.int32, (64, 192), 1)
    a = jnp.where(i < 32, i, i - 32)
    jj = jnp.where(j < 96, j, j - 96)
    w = taper(jj - 32 - a)
    high = w.astype(BF16).astype(F32)
    low = jnp.where(j < 96, w - high, 0.0)
    lat_k[...] = jnp.where(i < 32, high, low).astype(BF16)
    k = lax.broadcasted_iota(jnp.int32, (COLS, 2 * COLS), 0)
    n = lax.broadcasted_iota(jnp.int32, (COLS, 2 * COLS), 1)

    def lon(w, n):
        high = w.astype(BF16).astype(F32)
        return jnp.where(n < COLS, high, w - high).astype(BF16)

    out = jnp.where(n < COLS, n, n - COLS)
    own = lon(taper(k - out), n)
    k, n, out = k[:32], n[:32], out[:32]
    left, right = lon(taper(k - 32 - out), n), lon(taper(k + COLS - out), n)
    for s in range(4):
        lon_k[s, pl.ds(0, COLS), :] = own
        lon_k[s, pl.ds(COLS, 2 * COLS), :] = jnp.zeros((2 * COLS, 2 * COLS), BF16)
        lon_k[s, pl.ds(COLS + 32 * s, 32), :] = left
        lon_k[s, pl.ds(2 * COLS + 32 * s, 32), :] = right


def kernel(
    h_in, u_in, v_in, observed_in,
    h_out, u_out, v_out, inc,
    x, f, ps, pr, c, rc, lt, ls, lr, g1, lat_k, lon_k, coef, state, s_acc, sq, red,
    observed, strip, relay, relay_x, relay_p,
    load_sem, store_sem, halo_ss, halo_rs, halo_relay_rs, row_ss, row_rs, relay_rs, col_ss, col_rs, red_ss, red_rs,
):
    m = lax.axis_index("member")
    b = lax.axis_index("band")
    has_up = m > 0
    has_dn = m < NMEM - 1
    up = lax.rem(m + NMEM - 1, NMEM)
    dn = lax.rem(m + 1, NMEM)
    lf = lax.rem(b + NBAND - 1, NBAND)
    rt = lax.rem(b + 1, NBAND)

    core = lax.rem(m, 2)
    y = lax.rem(m // 2, 4)
    z_lo = m // 8
    xx = b // 2
    z = lax.rem(b, 2) * 2 + z_lo

    def at(core_, y_, x_, z_):
        return ((lax.rem(z_, 2) * 4 + y_) * 2 + core_, x_ * 2 + z_ // 2)

    stages = [
        [at(1 - core, y, xx, z)],
        [at(core, lax.rem(y + j, 4), xx, z) for j in (2, 1, 3)],
        [at(core, y, lax.rem(xx + j, 4), z) for j in (2, 1, 3)],
        [at(core, y, xx, lax.rem(z + j, 4)) for j in (2, 1, 3)],
    ]

    near = [(up, b), (dn, b), (m, lf), (m, rt), (up, lf), (up, rt), (dn, lf), (dn, rt)]
    mirror = (z_lo * 8 + 7 - lax.rem(m, 8), b)
    greet = near + [mirror] + [d for stage in stages for d in stage]
    barrier = pltpu.get_barrier_semaphore()
    for d in greet:
        pl.semaphore_signal(barrier, inc=1, device_id=d, device_id_type=MESH)

    loads = [
        pltpu.make_async_copy(src, dst, load_sem.at[k])
        for k, (src, dst) in enumerate((
            (h_in, x.at[0, pl.ds(0, MEMBERS), OWN]),
            (u_in, x.at[1, pl.ds(0, MEMBERS), OWN]),
            (v_in, x.at[2, pl.ds(0, MEMBERS), OWN]),
            (observed_in, observed),
        ))
    ]
    for copy in loads:
        copy.start()

    lane = lax.broadcasted_iota(jnp.int32, (ROWS, COLS), 1)

    def pack(g, count):
        left = jnp.zeros((ROWS, COLS), F32)
        right = jnp.zeros((ROWS, COLS), F32)
        for s in range(count):
            base = 16 * s
            i = g * 8 + s
            for field, lo, width in ((1, 0, 6), (0, 6, 5), (2, 11, 5)):
                value = x[field, i, OWN]
                where = (lane >= base + lo) & (lane < base + lo + width)
                left = jnp.where(where, pltpu.roll(value, base + lo, 1), left)
                right = jnp.where(where, pltpu.roll(value, (base + lo + width) % COLS, 1), right)
        ps[0, g, OWN] = left
        ps[1, g, OWN] = right

    def halo_copy(k, n, mean=False):
        members = pl.ds(MEAN, 1) if mean else pl.ds(n * 16, 16)
        groups = pl.ds(MEAN // 8, 1) if mean else pl.ds(n * 2, 2)
        src, dst, to = (
            (x.at[:, members, TOP], x.at[:, members, BELOW], (up, b)),
            (ps.at[:, groups, TOP], ps.at[:, groups, BELOW], (up, b)),
            (ps.at[0, groups, TOP], pr.at[1, groups, BELOW], (up, lf)),
            (ps.at[1, groups, TOP], pr.at[0, groups, BELOW], (up, rt)),
            (x.at[:, members, BOTTOM], x.at[:, members, ABOVE], (dn, b)),
            (ps.at[:, groups, BOTTOM], ps.at[:, groups, ABOVE], (dn, b)),
            (ps.at[0, groups, BOTTOM], pr.at[1, groups, ABOVE], (dn, lf)),
            (ps.at[1, groups, BOTTOM], pr.at[0, groups, ABOVE], (dn, rt)),
            (ps.at[0, groups, OWN], pr.at[1, groups, OWN], (m, lf)),
            (ps.at[1, groups, OWN], pr.at[0, groups, OWN], (m, rt)),
        )[k]
        return pltpu.make_async_remote_copy(
            src_ref=src, dst_ref=dst, send_sem=halo_ss.at[n, k], recv_sem=halo_rs.at[n, k],
            device_id=to, device_id_type=MESH,
        )

    def halo_relay_in(k, n):
        part = k % 4
        return pltpu.make_async_remote_copy(
            src_ref=(x.at[:, pl.ds(n * 16, 16), TOP if k < 4 else BOTTOM] if part == 0
                     else ps.at[:, pl.ds(n * 2, 2), TOP if k < 4 else BOTTOM]),
            dst_ref=(relay_x if part == 0 else relay_p).at[n // 2],
            send_sem=halo_ss.at[n, k], recv_sem=halo_relay_rs.at[n // 2, part],
            device_id=(0 if k < 4 else NMEM - 1, b), device_id_type=MESH,
        )

    def halo_relay_out(k, n):
        part = k % 4
        rows = BELOW if k < 4 else ABOVE
        return pltpu.make_async_remote_copy(
            src_ref=(relay_x if part == 0 else relay_p).at[n // 2],
            dst_ref=x.at[:, pl.ds(n * 16, 16), rows] if part == 0 else ps.at[:, pl.ds(n * 2, 2), rows],
            send_sem=halo_ss.at[n, k], recv_sem=halo_rs.at[n, k],
            device_id=(7 if k < 4 else 8, b), device_id_type=MESH,
        )

    def halo_forward(n):
        for end, ks in ((0, (0, 1)), (NMEM - 1, (4, 5))):

            @pl.when((m == end) & (lax.rem(n, 2) == 1))
            def _(ks=ks):
                for k in ks:
                    halo_relay_in(k, n).wait_recv()
                    halo_relay_out(k, n).start()

    def halo_start(n, mean=False):
        odd = False if mean else lax.rem(n, 2) == 1
        for there, source, ks in ((has_up, 8, range(0, 4)), (has_dn, 7, range(4, 8))):
            away = (m == source) & odd

            @pl.when(there & jnp.logical_not(away))
            def _(ks=ks):
                for k in ks[:2]:
                    halo_copy(k, n, mean).start()

            if not mean:

                @pl.when(away)
                def _(ks=ks):
                    for k in ks[:2]:
                        halo_relay_in(k, n).start()

            @pl.when(there)
            def _(ks=ks):
                for k in ks[2:]:
                    halo_copy(k, n, mean).start()

        for k in (8, 9):
            halo_copy(k, n, mean).start()

    def halo_wait(n, mean=False):
        @pl.when(has_up)
        def _():
            for k in range(4, 8):
                halo_copy(k, n, mean).wait_recv()
            for k in range(0, 4):
                halo_copy(k, n, mean).wait_send()

        @pl.when(has_dn)
        def _():
            for k in range(0, 4):
                halo_copy(k, n, mean).wait_recv()
            for k in range(4, 8):
                halo_copy(k, n, mean).wait_send()

        for k in (8, 9):
            halo_copy(k, n, mean).wait_recv()
            halo_copy(k, n, mean).wait_send()

        if not mean:
            for end, ks in ((0, (0, 1)), (NMEM - 1, (4, 5))):

                @pl.when((m == end) & (lax.rem(n, 2) == 1))
                def _(ks=ks):
                    for k in ks:
                        halo_relay_out(k, n).wait_send()

    def send_halo(n, carry):
        for gg in range(2):
            pack(2 * n + gg, 8)
        halo_start(n)
        return carry

    for copy in loads:
        copy.wait()
    for gg in range(2):
        pack(gg, 8)
    pl.semaphore_wait(barrier, len(greet))
    halo_start(0)

    for k in range(3):
        x[k, MEAN, OWN] = lax.fori_loop(
            0, MEMBERS, lambda i, total, k=k: total + x[k, i, OWN], jnp.zeros((ROWS, COLS), F32), unroll=8
        ) * (1.0 / MEMBERS)
    pack(MEAN // 8, 1)
    halo_start(NHALO, True)

    lax.fori_loop(1, NHALO, send_halo, 0)

    def clear(halo, side):
        x[:, :, halo, :] = jnp.zeros((3, MEMBERS + 8, 6, COLS), F32)
        ps[:, :, halo, :] = jnp.zeros((2, GROUPS, 6, COLS), F32)
        pr[:, :, halo, :] = jnp.zeros((2, GROUPS, 6, COLS), F32)
        for it in range(2):
            rc[it, side] = jnp.zeros((MEMBERS, ROWS, COLS), F32)

    @pl.when(m == 0)
    def _():
        clear(ABOVE, 0)

    @pl.when(m == NMEM - 1)
    def _():
        clear(BELOW, 1)

    build_tapers(lat_k, lon_k)

    tile = lax.broadcasted_iota(jnp.int32, (8, COLS), 0)
    column = lax.broadcasted_iota(jnp.int32, (8, COLS), 1)
    inside = [
        ((6 * tile + j >= 8) | has_up) & ((6 * tile + j < 40) | has_dn) for j in range(6)
    ]
    place = lax.rem(column, 16)
    edge = (column < 6) | (column >= COLS - 6)

    def lon_diff(q):
        return [pltpu.roll(w, COLS - 1, 1) - pltpu.roll(w, 1, 1) for w in q]

    def lat_diff(q):
        out = []
        for first in range(0, len(q), 6):
            part = q[first:first + 6]
            after = part[1:] + [pltpu.roll(part[0], 7, 0)]
            before = [pltpu.roll(part[5], 1, 0)] + part[:5]
            out += [p - w for p, w in zip(after, before)]
        return out

    def advance(hh, uu, vv, keep):
        six = range(len(hh))
        for _ in range(STEPS):
            du, dv = lon_diff(uu), lat_diff(vv)
            hn = [jnp.where(keep[j % 6], hh[j] - 0.2 * (du[j] + dv[j]), 0.0) for j in six]
            dx, dy = lon_diff(hn), lat_diff(hn)
            un = [uu[j] + 0.1 * vv[j] - 0.2 * dx[j] for j in six]
            vn = [jnp.where(inside[j % 6], vv[j] - 0.1 * uu[j] - 0.2 * dy[j], 0.0) for j in six]
            hh, uu, vv = hn, un, vn
        return hh, uu, vv

    def strided(j):
        return pl.ds(j, 8, stride=6)

    def strips(g):
        keep = [w & (place < 12) for w in inside]

        def side(sign, u_shift, h_shift, v_shift, start, u_start):
            far = [pr[sign, g, strided(j)] - ps[1 - sign, g, strided(j)] for j in range(6)]

            def cut(shift, first, width):
                where = (place >= first) & (place < first + width)
                return [jnp.where(where, pltpu.roll(w, shift % COLS, 1) if shift else w, 0.0) for w in far]

            return cut(h_shift, start, 5), cut(u_shift, u_start, 6), cut(v_shift, start, 5)

        left = side(0, 0, -5, -10, 1, 0)
        right = side(1, 6, 0, -5, 6, 6)
        out = advance(*[p + w for p, w in zip(left, right)], keep)
        for k in range(3):
            for j in range(6):
                strip[k, j] = jnp.where(place < 6, out[k][6 + j], out[k][j])

    def forecast(first, s, count):
        out = advance(
            *[[x[k, first + t, strided(j)] for t in range(count) for j in range(6)] for k in range(3)], inside
        )
        for t in range(count):
            shift = (2 * COLS - 6 - 16 * (s + t)) % COLS
            for k in range(3):
                for j in range(6):
                    more = jnp.where(edge, pltpu.roll(strip[k, j], shift, 1), 0.0)
                    f[k, first + t, strided(j)] = out[k][6 * t + j] + more

    halo_wait(NHALO, True)
    strips(MEAN // 8)
    forecast(MEAN, 0, 1)
    mean = [f[k, MEAN, OWN] for k in range(3)]
    for k in range(3):
        state[k] = mean[k]

    def set_coefficients(sh, su, sv):
        residual = observed[pl.ds(ROWS, ROWS)] * (observed[pl.ds(0, ROWS)] - sh - 0.15 * (su * su + sv * sv))
        coef[0] = residual
        coef[1] = 0.3 * su * residual
        coef[2] = 0.3 * sv * residual

    set_coefficients(*mean)

    def row_copy(it, k, n):
        members = pl.ds(n * CHUNK, CHUNK)
        return pltpu.make_async_remote_copy(
            src_ref=c.at[members], dst_ref=rc.at[it, 1 - k, members],
            send_sem=row_ss.at[it, k, n], recv_sem=row_rs.at[it, k, n],
            device_id=near[k], device_id_type=MESH,
        )

    def by_relay(k, n):
        return (m == (8 if k == 0 else 7)) & (lax.rem(n, 2) == 1)

    def at_relay(k, n):
        return (m == (0 if k == 0 else NMEM - 1)) & (lax.rem(n, 2) == 1)

    def relay_in(it, k, n):
        return pltpu.make_async_remote_copy(
            src_ref=c.at[pl.ds(n * CHUNK, CHUNK)], dst_ref=relay.at[it, n // 2],
            send_sem=row_ss.at[it, k, n], recv_sem=relay_rs.at[it, n // 2],
            device_id=(0 if k == 0 else NMEM - 1, b), device_id_type=MESH,
        )

    def relay_out(it, k, n):
        return pltpu.make_async_remote_copy(
            src_ref=relay.at[it, n // 2], dst_ref=rc.at[it, 1 - k, pl.ds(n * CHUNK, CHUNK)],
            send_sem=row_ss.at[it, k, n], recv_sem=row_rs.at[it, k, n],
            device_id=(7 if k == 0 else 8, b), device_id_type=MESH,
        )

    def row_start(it, n):
        for k, there in ((0, has_up), (1, has_dn)):
            pl.when(there & jnp.logical_not(by_relay(k, n)))(row_copy(it, k, n).start)
            pl.when(by_relay(k, n))(relay_in(it, k, n).start)

    def relay_forward(it, n):
        for k in range(2):

            @pl.when(at_relay(k, n))
            def _(k=k):
                relay_in(it, k, n).wait_recv()
                relay_out(it, k, n).start()

    def row_wait(it, n):
        @pl.when(has_up)
        def _():
            row_copy(it, 1, n).wait_recv()

        @pl.when(has_dn)
        def _():
            row_copy(it, 0, n).wait_recv()

    def row_sent(it, n):
        for k, there in ((0, has_up), (1, has_dn)):
            pl.when(there | at_relay(k, n))(row_copy(it, k, n).wait_send)

    def col_copy(it, k, n):
        quads = pl.ds(n * QUADS, QUADS)
        return pltpu.make_async_remote_copy(
            src_ref=ls.at[k, quads], dst_ref=lr.at[it, 1 - k, quads],
            send_sem=col_ss.at[it, k, n], recv_sem=col_rs.at[it, k, n],
            device_id=near[2 + k], device_id_type=MESH,
        )

    scale = 1.0 / math.sqrt(MEMBERS - 1.0)

    def taper_rows(it, n):
        row_wait(it, n)
        pl.when(n + 1 < NCHUNK)(lambda: relay_forward(it, n + 1))

        for qq in range(QUADS):
            q = n * QUADS + qq
            parts_high, parts_low = [], []
            for ref_part in range(3):
                wide = []
                for s in range(4):
                    i = q * 4 + s
                    wide.append(rc[it, 0, i] if ref_part == 0 else (c[i] if ref_part == 1 else rc[it, 1, i]))
                high, low = split(jnp.concatenate(wide, axis=1))
                parts_high.append(high)
                parts_low.append(low)
            right_side = jnp.concatenate(parts_high + parts_low, axis=0)
            both = jnp.dot(lat_k[...], right_side, preferred_element_type=F32)
            lat = both[:32] + both[32:]
            to_left = jnp.zeros((ROWS, COLS), F32)
            to_right = jnp.zeros((ROWS, COLS), F32)
            for s in range(4):
                part = lat[:, s * COLS:(s + 1) * COLS]
                lt[s, q] = part
                where = (lane >= 32 * s) & (lane < 32 * s + 32)
                to_left = jnp.where(where, pltpu.roll(part, 32 * s, 1) if s else part, to_left)
                to_right = jnp.where(where, pltpu.roll(part, 32 * s + 32, 1) if s < 3 else part, to_right)
            ls[0, q] = to_left
            ls[1, q] = to_right

        for k in range(2):
            col_copy(it, k, n).start()

    def first_chunk(n, carry):
        halo_wait(n)
        pl.when(n + 1 < NHALO)(lambda: halo_forward(n + 1))
        for gg in range(2):
            g = n * 2 + gg
            strips(g)

            for s in range(0, 8, TOGETHER):
                first = g * 8 + s
                forecast(first, s, TOGETHER)
                for t in range(TOGETHER):
                    i = first + t
                    total = None
                    for k in range(3):
                        anomaly = (f[k, i, OWN] - state[k]) * scale
                        x[k, i, OWN] = anomaly
                        term = anomaly * coef[k]
                        total = term if total is None else total + term
                    c[i] = total
            row_start(0, g)

        @pl.when(n >= LAG)
        def _():
            for gg in range(2):
                taper_rows(0, 2 * (n - LAG) + gg)

        return carry

    lax.fori_loop(0, NHALO, first_chunk, 0)

    stores = [
        pltpu.make_async_copy(f.at[k, pl.ds(0, MEMBERS), OWN], dst, store_sem.at[k])
        for k, dst in enumerate((h_out, u_out, v_out))
    ]
    for copy in stores:
        copy.start()

    def taper_cols(it, n, factor):
        for k in range(2):
            col_copy(it, k, n).wait_recv()
        quads = pl.ds(n * QUADS, QUADS)
        size = QUADS * ROWS
        lh, ll = split(lr[it, 0, quads].reshape(size, COLS))
        rhh, rl = split(lr[it, 1, quads].reshape(size, COLS))
        totals = [None] * 4
        for s in range(4):
            mh, ml = split(lt[s, quads].reshape(size, COLS))
            a = jnp.dot(jnp.concatenate([mh, lh, rhh], axis=1), lon_k[s], preferred_element_type=F32)
            d = jnp.dot(jnp.concatenate([ml, ll, rl], axis=1), lon_k[s, :, pl.ds(0, 128)], preferred_element_type=F32)
            g = (a[:, :COLS] + a[:, COLS:] + d).reshape(QUADS, ROWS, COLS)
            if it == 0:
                g1[s, quads] = g
            else:
                g = factor * g1[s, quads] - g
            for qq in range(QUADS):
                i = (n * QUADS + qq) * 4 + s
                part = g[qq]
                terms = [x[k, i, OWN] * part for k in range(3)] + [part * part]
                totals = [t if o is None else o + t for o, t in zip(totals, terms)]
        for k in range(3):
            s_acc[it, k] += totals[k]
        sq[...] += totals[3]

    def localize(it, factor):
        early, behind = (NCHUNK - 2 * LAG, BEHIND) if it == 0 else (0, SKEW)

        def body(n, carry):
            @pl.when(n + early < NCHUNK)
            def _():
                taper_rows(it, n + early)

            @pl.when(n >= behind)
            def _():
                taper_cols(it, n - behind, factor)

            return carry

        lax.fori_loop(0, NCHUNK + behind, body, 0)

    def sum_all(it):
        value = sq[...]
        value = value[:8] + value[8:16] + value[16:24] + value[24:]
        slot = 0
        started = []
        for stage in stages:
            red[it, slot] = value
            copies = [
                pltpu.make_async_remote_copy(
                    src_ref=red.at[it, slot], dst_ref=red.at[it, slot + 1 + j],
                    send_sem=red_ss.at[it, slot + j], recv_sem=red_rs.at[it, slot + j],
                    device_id=d, device_id_type=MESH,
                )
                for j, d in enumerate(stage)
            ]
            for copy in copies:
                copy.start()
            for copy in copies:
                copy.wait_recv()
            for j in range(len(stage)):
                value = value + red[it, slot + 1 + j]
            started.extend(copies)
            slot += 1 + len(stage)
        for copy in started:
            copy.wait_send()
        total = jnp.sum(jnp.sum(value, axis=0, keepdims=True), axis=1, keepdims=True)
        return observed[pl.ds(2 * ROWS + 8 * it, 1), pl.ds(0, 1)] / jnp.sqrt(total / CELLS + 1e-6)

    for it in range(2):
        for k in range(3):
            s_acc[it, k] = jnp.zeros((ROWS, COLS), F32)
    sq[...] = jnp.zeros((ROWS, COLS), F32)
    localize(0, None)
    factor1 = sum_all(0)

    def sent(n, carry):
        row_sent(0, n)
        for k in range(2):
            col_copy(0, k, n).wait_send()
        return carry

    lax.fori_loop(0, NCHUNK, sent, 0)
    sq[...] = jnp.zeros((ROWS, COLS), F32)
    set_coefficients(*[state[k] + factor1 * s_acc[0, k] for k in range(3)])

    def second_chunk(n, carry):
        def one(j, carry2):
            i = n * CHUNK + j
            c[i] = x[0, i, OWN] * coef[0] + x[1, i, OWN] * coef[1] + x[2, i, OWN] * coef[2]
            return carry2

        lax.fori_loop(0, CHUNK, one, 0, unroll=4)
        row_start(1, n)
        return carry

    lax.fori_loop(0, NCHUNK, second_chunk, 0)
    localize(1, factor1)
    factor2 = sum_all(1)
    for k in range(3):
        inc[k] = factor1 * s_acc[0, k] - factor2 * s_acc[1, k]

    def sent2(n, carry):
        row_sent(1, n)
        for k in range(2):
            col_copy(1, k, n).wait_send()
        return carry

    lax.fori_loop(0, NCHUNK, sent2, 0)
    for copy in stores:
        copy.wait()


def per_device(height, east, north, obs_value, obs_mask, obs_precision, step_sizes):
    block = (MEMBERS, ROWS, COLS)
    vmem = pl.BlockSpec(memory_space=pltpu.VMEM)
    anyspace = pl.BlockSpec(memory_space=pl.ANY)
    dma = pltpu.SemaphoreType.DMA
    steps = jnp.broadcast_to((step_sizes.astype(F32) / 64.0)[:, None, None], (2, 8, COLS))
    observed = jnp.concatenate(
        [obs_value, obs_mask.astype(F32) * obs_precision, steps.reshape(16, COLS)], axis=0
    )
    h, u, v, inc = pl.pallas_call(
        kernel,
        name="analysis",
        out_shape=[jax.ShapeDtypeStruct(block, F32)] * 3 + [jax.ShapeDtypeStruct((3, ROWS, COLS), F32)],
        in_specs=[pl.BlockSpec(memory_space=pltpu.HBM)] * 4,
        out_specs=[anyspace] * 3 + [vmem],
        scratch_shapes=[
            pltpu.VMEM((3, MEMBERS + 8, 48, COLS), F32),
            pltpu.VMEM((3, MEMBERS + 1, 48, COLS), F32),
            pltpu.VMEM((2, GROUPS, 48, COLS), F32),
            pltpu.VMEM((2, GROUPS, 48, COLS), F32),
            pltpu.VMEM(block, F32),
            pltpu.VMEM((2, 2) + block, F32),
            pltpu.VMEM((4, MEMBERS // 4, ROWS, COLS), F32),
            pltpu.VMEM((2, MEMBERS // 4, ROWS, COLS), F32),
            pltpu.VMEM((2, 2, MEMBERS // 4, ROWS, COLS), F32),
            pltpu.VMEM((4, MEMBERS // 4, ROWS, COLS), F32),
            pltpu.VMEM((64, 192), BF16),
            pltpu.VMEM((4, 384, 256), BF16),
            pltpu.VMEM((3, ROWS, COLS), F32),
            pltpu.VMEM((3, ROWS, COLS), F32),
            pltpu.VMEM((2, 3, ROWS, COLS), F32),
            pltpu.VMEM((ROWS, COLS), F32),
            pltpu.VMEM((2, 14, 8, COLS), F32),
            pltpu.VMEM((2 * ROWS + 16, COLS), F32),
            pltpu.VMEM((3, 6, 8, COLS), F32),
            pltpu.VMEM((2, NCHUNK // 2, CHUNK, ROWS, COLS), F32),
            pltpu.VMEM((NHALO // 2, 3, 16, 6, COLS), F32),
            pltpu.VMEM((NHALO // 2, 2, 2, 6, COLS), F32),
            dma((4,)), dma((3,)),
            dma((NHALO + 1, 10)), dma((NHALO + 1, 10)), dma((NHALO // 2, 2)),
            dma((2, 2, NCHUNK)), dma((2, 2, NCHUNK)), dma((2, NCHUNK // 2)),
            dma((2, 2, NCHUNK)), dma((2, 2, NCHUNK)),
            dma((2, 14)), dma((2, 14)),
        ],
        compiler_params=pltpu.CompilerParams(
            collective_id=0, has_side_effects=True, vmem_limit_bytes=50 << 20
        ),
    )(height, east, north, observed)
    return h + inc[0], u + inc[1], v + inc[2]


def solution(mesh):
    spec3 = P(None, "member", "band")
    spec2 = P("member", "band")
    return jax.shard_map(
        per_device,
        mesh=mesh,
        in_specs=(spec3, spec3, spec3, spec2, spec2, spec2, P()),
        out_specs=(spec3, spec3, spec3),
        check_vma=False,
    )
```
